32 devices in a mesh: space: 8 (over z, y), step: 4 (over x, core).
Axes of the slice: x: 2, y: 2, z: 4, core: 2. Of those that a mesh axis runs over, the one named last changes fastest.
Arguments:
- image: float32 [3, 128, 256], P(None, 'space'), may hold values from -6 to 6
- baseline: float32 [3, 128, 256], P(None, 'space'), may hold values from -0.5 to 0.5
- w_first: float32 [64, 3, 3, 3], replicated, may hold values from -1.25 to 1.25
- w_rest: float32 [3, 64, 64, 3, 3], replicated, may hold values from -0.375 to 0.375
- target: float32 [64, 128, 256], P(None, 'space'), may hold values from -6 to 6
Outputs:
- attribution: float32 [3, 128, 256], P(None, 'space')
The draws below stay inside these ranges and needn't reach their ends.
All inputs are finite; a program needn't handle non-finite values.
Results may differ from the reference program's by a relative error of at most 0.0001.
Values sent between devices are 32-bit elements; how exact they have to be, the bound alone decides.
No kernel may reach another device: no remote copies, remote signals or barrier semaphores. Data moves between devices by JAX's collectives and lax.ppermute only.
A program may use at most 64 MiB of HBM per device.

```python
import jax
import jax.numpy as jnp
from jax import lax

CIN = 3
CH = 64
LAYERS = 4
WIDTH = 256
TILE_ROWS = 128
STEPS = 4


def levels(stream_key, shape, cuts, low, largest):
    gain, own = 1.0, jax.random.fold_in(stream_key, 6)
    for dim, parts in cuts:
        draws = jnp.exp(jax.random.uniform(jax.random.fold_in(own, dim), (parts,), jnp.float32, low / len(cuts), largest / len(cuts)))
        gain = gain * jnp.repeat(draws, shape[dim] // parts).reshape([-1 if axis == dim else 1 for axis in range(len(shape))])
    return gain


def normal_values(own_key, dims, scale, bound, cuts=(), kind=jnp.bfloat16):
    values = scale * jax.random.normal(own_key, dims, jnp.float32)
    if cuts:
        values = values * levels(own_key, dims, cuts, -0.22, 0.18)
    return jnp.clip(values, -bound, bound).astype(kind)


def setup_inputs(seed: int = 0) -> dict:
    key_list = jax.random.split(jax.random.key(seed), 6)
    image = normal_values(key_list[0], (CIN, TILE_ROWS, WIDTH), 1.0, 6.0, ((1, 8),), jnp.float32)
    baseline = jnp.clip(jax.random.uniform(key_list[1], (CIN, TILE_ROWS, WIDTH), jnp.float32, -0.5, 0.5) * levels(key_list[1], (CIN, TILE_ROWS, WIDTH), ((1, 8),), -0.4, 0.0), -0.5, 0.5)
    w_first = normal_values(key_list[2], (CH, CIN, 3, 3), (CIN * 9) ** -0.5, 1.25, (), jnp.float32)
    w_rest = normal_values(key_list[3], (LAYERS - 1, CH, CH, 3, 3), (CH * 9 // 2) ** -0.5, 0.375, (), jnp.float32)
    target = normal_values(key_list[4], (CH, TILE_ROWS, WIDTH), 1.0, 6.0, ((1, 8),), jnp.float32)
    return {"image": image, "baseline": baseline, "w_first": w_first, "w_rest": w_rest, "target": target}


def conv_same(field, kernel):
    return lax.conv_general_dilated(field[None], kernel, (1, 1), ((1, 1), (1, 1)), dimension_numbers=('NCHW', 'OIHW', 'NCHW'), precision=lax.Precision.HIGHEST)[0]

def reference(image, baseline, w_first, w_rest, target):
    difference = image - baseline

    def score(inputs):
        current = inputs
        for layer_index in range(LAYERS):
            kernel = w_first if layer_index == 0 else w_rest[layer_index - 1]
            pre = conv_same(current, kernel)
            current = jax.nn.silu(pre) if layer_index < LAYERS - 1 else pre
        return jnp.sum(current * target)

    def add_step(summed, position):
        fraction = (position.astype(jnp.float32) + 0.5) / STEPS
        gradient = jax.grad(score)(baseline + fraction * difference)
        return (summed + gradient, None)
    summed, _ = lax.scan(add_step, jnp.zeros_like(image), jnp.arange(STEPS, dtype=jnp.int32))
    return difference * summed / STEPS
```

```python
import jax
import jax.numpy as jnp
from jax import lax
from jax.experimental import pallas as pl
from jax.experimental.pallas import tpu as pltpu
from jax.sharding import PartitionSpec as P

F32, BF16 = jnp.float32, jnp.bfloat16
HALO_X, HALO_T = 6, 4


def dot(a, b):
    return jnp.dot(a, b, preferred_element_type=F32)


def split(value):
    high = value.astype(BF16)
    return high, (value - high.astype(F32)).astype(BF16)


def shift_cols(value, by):
    width = value.shape[-1]
    col = lax.broadcasted_iota(jnp.int32, value.shape, value.ndim - 1)
    edge = 0 if by > 0 else width - 1
    return jnp.where(col == edge, 0.0, pltpu.roll(value, by % width, value.ndim - 1))


def combine(y, rows):
    return y[rows : 2 * rows] + shift_cols(y[:rows], 1) + shift_cols(y[2 * rows : 3 * rows], -1)


def silu_and_slope(pre):
    sig = 1.0 / (1.0 + jnp.exp(-pre))
    act = pre * sig
    return act, sig + act * (1.0 - sig)


def conv_row(weights, high, low, index):
    stack = lambda ref: ref[index : index + 3].reshape(3 * ref.shape[1], ref.shape[2])
    upper, lower = stack(high), stack(low)
    return dot(weights, jnp.concatenate([upper, upper, lower], 0))


def make_kernel(rows, half, channels, width, total_rows):
    def kernel(info, x_own, x_halo, t_own, t_halo, w1, wf, wb, w1t, out, xs, a1h, a1l, a2h, a2l, th, tl, d3h, d3l, d2h, d2l, d1h, d1l, s1, s2, s3):
        upper_half = info[0] == 0
        first = info[1]
        own0 = info[0] * half

        def keep(value, local):
            if 0 <= local < half:
                return value
            row = first + local
            return jnp.where((row >= 0) & (row < total_rows), value, 0.0)

        def window(own, halo, local, count, depth):
            at = lambda r: own[:, r, :]
            if local < 0:
                return jnp.where(upper_half, halo[local + depth], at(local + half))
            if local >= half:
                return jnp.where(upper_half, at(local), halo[local - half])
            return at(own0 + local)

        for j in range(half + 2 * HALO_X):
            x = window(x_own, x_halo, j - HALO_X, 8, HALO_X)
            taps = jnp.concatenate([shift_cols(x, 1), x, shift_cols(x, -1)], 0)
            high = taps.astype(BF16).astype(F32)
            xs[j] = jnp.concatenate([high, taps - high], 0).astype(BF16)
        for j in range(half + 2 * HALO_T):
            th[j], tl[j] = split(window(t_own, t_halo, j - HALO_T, channels, HALO_T))
        for j in range(half + 10):
            stack = xs[j : j + 3].reshape(3 * xs.shape[1], width)
            pre = dot(w1[...], jnp.concatenate([stack, stack], 0))
            local = j - 5
            for s in range(2):
                act, slope = silu_and_slope(pre[s * channels : (s + 1) * channels])
                a1h[s, j], a1l[s, j] = split(keep(act, local))
                if -1 <= local <= half:
                    s1[s, local + 1] = keep(slope, local)
        for j in range(half + 8):
            local = j - 4
            for s in range(2):
                pre = combine(conv_row(wf[0], a1h.at[s], a1l.at[s], j), channels)
                act, slope = silu_and_slope(pre)
                a2h[s, j], a2l[s, j] = split(keep(act, local))
                if -2 <= local <= half + 1:
                    s2[s, local + 2] = keep(slope, local)
        for j in range(half + 6):
            local = j - 3
            grad = combine(conv_row(wb[2], th, tl, j), channels)
            for s in range(2):
                pre = combine(conv_row(wf[1], a2h.at[s], a2l.at[s], j), channels)
                act, slope = silu_and_slope(pre)
                d3h[s, j], d3l[s, j] = split(keep(grad * slope, local))
        for j in range(half + 4):
            for s in range(2):
                grad = combine(conv_row(wb[1], d3h.at[s], d3l.at[s], j), channels)
                d2h[s, j], d2l[s, j] = split(grad * s2[s, j])
        for j in range(half + 2):
            for s in range(2):
                grad = combine(conv_row(wb[0], d2h.at[s], d2l.at[s], j), channels)
                d1h[s, j], d1l[s, j] = split(grad * s1[s, j])
        for j in range(half):
            total = 0.0
            for s in range(2):
                total = total + conv_row(w1t[...], d1h.at[s], d1l.at[s], j)
            out[j] = combine(total, 8)

    return kernel


def parts(value):
    high = lax.reduce_precision(value, 8, 7)
    low = (value - high).astype(BF16)
    high = high.astype(BF16)
    return high, low


def wide(matrix):
    high, low = parts(matrix)
    return jnp.concatenate([high, low, high], -1)


def lower_weights(w_first, w_rest):
    layers, channels = w_rest.shape[0], w_rest.shape[1]
    colours = w_first.shape[1]
    n = 3 * channels
    forward = wide(w_rest.transpose(0, 4, 1, 3, 2).reshape(layers, n, n))
    flipped = jnp.flip(w_rest, (3, 4))
    backward = wide(flipped.transpose(0, 4, 2, 3, 1).reshape(layers, n, n))
    first = w_first.transpose(0, 2, 3, 1)
    first = jnp.pad(first, ((0, 0),) * 3 + ((0, 4 - colours),))
    blank = jnp.zeros_like(first)
    both = jnp.stack([jnp.stack([first, blank], 3), jnp.stack([blank, first], 3)], 0)
    both = both.reshape(2 * channels, 3, 24)
    high, low = parts(both)
    one = jnp.concatenate([high, high], -1).reshape(2 * channels, 144)
    two = jnp.concatenate([low, jnp.zeros_like(low)], -1).reshape(2 * channels, 144)
    w1 = jnp.concatenate([one, two], -1)
    back = jnp.flip(w_first, (2, 3)).transpose(3, 1, 2, 0)
    back = jnp.pad(back, ((0, 0), (0, 8 - colours), (0, 0), (0, 0))).reshape(24, n)
    return w1, forward, backward, wide(back)


def body(image, baseline, w_first, w_rest, target):
    colours, rows, width = image.shape
    channels = target.shape[0]
    half = rows // 2
    space_n, step_n = lax.axis_size("space"), lax.axis_size("step")
    space, step = lax.axis_index("space"), lax.axis_index("step")
    side, group = step % 2, step // 2
    difference = image - baseline
    fraction = (group * 2).astype(F32) + 0.5
    pad = jnp.zeros((1, rows, width), F32)
    x_own = jnp.concatenate(
        [baseline + fraction / step_n * difference, pad, baseline + (fraction + 1.0) / step_n * difference, pad], 0
    )
    pairs = []
    for i in range(space_n):
        for s in range(step_n):
            source = i + 1 if s % 2 else i - 1
            if 0 <= source < space_n:
                pairs.append((source * step_n + s, i * step_n + s))

    def edge(array, depth):
        picked = jnp.where(side == 0, array[:, rows - depth :], array[:, :depth])
        return lax.ppermute(picked.transpose(1, 0, 2), ("space", "step"), pairs)

    x_halo = edge(x_own, HALO_X)
    t_halo = edge(target, HALO_T)
    weights = lower_weights(w_first, w_rest)
    info = jnp.stack([side, space * rows + side * half]).astype(jnp.int32)
    kernel = make_kernel(rows, half, channels, width, rows * space_n)
    vmem = pl.BlockSpec(memory_space=pltpu.VMEM)
    maps = lambda count, kind: pltpu.VMEM((2, count, channels, width), kind)
    single = pltpu.VMEM((half + 8, channels, width), BF16)
    y = pl.pallas_call(
        kernel,
        out_shape=jax.ShapeDtypeStruct((half, 8, width), F32),
        in_specs=[pl.BlockSpec(memory_space=pltpu.SMEM)] + [vmem] * 8,
        out_specs=vmem,
        scratch_shapes=[pltpu.VMEM((half + 12, 48, width), BF16)]
        + [maps(half + 10, BF16)] * 2
        + [maps(half + 8, BF16)] * 2
        + [single] * 2
        + [maps(half + 6, BF16)] * 2
        + [maps(half + 4, BF16)] * 2
        + [maps(half + 2, BF16)] * 2
        + [maps(half + 2, F32), maps(half + 4, F32), maps(1, F32)],
        compiler_params=pltpu.CompilerParams(vmem_limit_bytes=48 << 20),
        name="attribution",
    )(info, x_own, x_halo, target, t_halo, *weights)
    y = y.transpose(1, 0, 2)[:colours]

    def shifted(k):
        return lax.ppermute(y, "step", [(i, (i + k) % step_n) for i in range(step_n)])

    same = [y]
    other = []
    for k in range(1, step_n):
        (other if k % 2 else same).append(shifted(k))
    if step_n > 4:
        order = lax.broadcasted_iota(jnp.int32, (2, 1, 1, 1), 0)
        halves = lax.psum(jnp.where(order == side, y[None], 0.0), "step")
        whole = jnp.concatenate([halves[0], halves[1]], 1)
    else:
        mine, theirs = sum(same[1:], same[0]), sum(other[1:], other[0])
        whole = jnp.where(side == 0, jnp.concatenate([mine, theirs], 1), jnp.concatenate([theirs, mine], 1))
    return difference * whole / step_n


def solution(mesh):
    in_specs = (P(None, "space", None), P(None, "space", None), P(), P(), P(None, "space", None))
    out_specs = P(None, "space", None)
    return jax.shard_map(body, mesh=mesh, in_specs=in_specs, out_specs=out_specs, check_vma=False)
```

```python
import jax
import jax.numpy as jnp
from jax import lax
from jax.experimental import pallas as pl
from jax.experimental.pallas import tpu as pltpu
from jax.sharding import PartitionSpec as P

F32, BF16 = jnp.float32, jnp.bfloat16
HALO_X, HALO_T = 6, 4
VMEM = pl.BlockSpec(memory_space=pltpu.VMEM)
SMEM = pl.BlockSpec(memory_space=pltpu.SMEM)


def dot(a, b):
    return jnp.dot(a, b, preferred_element_type=F32)


def split(value):
    high = value.astype(BF16)
    return high, (value - high.astype(F32)).astype(BF16)


def shift_cols(value, by):
    width = value.shape[-1]
    col = lax.broadcasted_iota(jnp.int32, value.shape, value.ndim - 1)
    edge = 0 if by > 0 else width - 1
    return jnp.where(col == edge, 0.0, pltpu.roll(value, by % width, value.ndim - 1))


def combine(y, rows):
    return y[rows : 2 * rows] + shift_cols(y[:rows], 1) + shift_cols(y[2 * rows : 3 * rows], -1)


def silu_and_slope(pre):
    sig = 1.0 / (1.0 + jnp.exp(-pre))
    act = pre * sig
    return act, sig + act * (1.0 - sig)


def conv_row(weights, high, low, index):
    stack = lambda ref: ref[index : index + 3].reshape(3 * ref.shape[1], ref.shape[2])
    upper, lower = stack(high), stack(low)
    return dot(weights, jnp.concatenate([upper, upper, lower], 0))


class Maps:
    def __init__(self, refs, base):
        self.high, self.low = refs
        self.base = base

    def put(self, step, row, value):
        self.high[step, row - self.base], self.low[step, row - self.base] = split(value)

    def conv(self, weights, step, row):
        return conv_row(weights, self.high.at[step], self.low.at[step], row - 1 - self.base)

    def copy(self, refs, row, count):
        for part, ref in zip((self.high, self.low), refs):
            ref[...] = part[:, row - self.base : row - self.base + count]

    def load(self, refs, row, count):
        for part, ref in zip((self.high, self.low), refs):
            part[:, row - self.base : row - self.base + count] = ref[...]


def run(spans, weights, xs, x_base, maps, slopes, x_row, t_row, keep, emit, channels, width):
    w1, wf, wb, w1t = weights
    a1, a2, t, d3, d2, d1 = maps
    s1, s1_base, s2, s2_base = slopes
    rows = lambda name: range(spans[name][0], spans[name][1] + 1)
    inside = lambda name, row: spans[name][0] <= row <= spans[name][1]
    for j in rows("x"):
        x = x_row(j)
        taps = jnp.concatenate([shift_cols(x, 1), x, shift_cols(x, -1)], 0)
        high = taps.astype(BF16).astype(F32)
        xs[j - x_base] = jnp.concatenate([high, taps - high], 0).astype(BF16)
    for j in rows("t"):
        t.put(0, j, t_row(j))
    for j in rows("a1"):
        stack = xs[j - 1 - x_base : j + 2 - x_base].reshape(3 * xs.shape[1], width)
        pre = dot(w1[...], jnp.concatenate([stack, stack], 0))
        for s in range(2):
            act, slope = silu_and_slope(pre[s * channels : (s + 1) * channels])
            a1.put(s, j, keep(act, j))
            if inside("s1", j):
                s1[s, j - s1_base] = keep(slope, j)
    for j in rows("a2"):
        for s in range(2):
            act, slope = silu_and_slope(combine(a1.conv(wf[0], s, j), channels))
            a2.put(s, j, keep(act, j))
            if inside("s2", j):
                s2[s, j - s2_base] = keep(slope, j)
    for j in rows("d3"):
        grad = combine(t.conv(wb[2], 0, j), channels)
        for s in range(2):
            _, slope = silu_and_slope(combine(a2.conv(wf[1], s, j), channels))
            d3.put(s, j, keep(grad * slope, j))
    for j in rows("d2"):
        for s in range(2):
            d2.put(s, j, combine(d3.conv(wb[1], s, j), channels) * s2[s, j - s2_base])
    for j in rows("d1"):
        for s in range(2):
            d1.put(s, j, combine(d2.conv(wb[0], s, j), channels) * s1[s, j - s1_base])
    for j in rows("out"):
        emit(j, combine(d1.conv(w1t[...], 0, j) + d1.conv(w1t[...], 1, j), 8))


def prepare(side, w, w_first, w1, wf, wb, w1t, channels, colours):
    tap = lambda dy: jnp.where(side == 1, 2 - dy, dy)

    def halves(pieces):
        high = [p.astype(BF16).astype(F32) for p in pieces]
        return high, [p - h for p, h in zip(pieces, high)]

    def wide(pieces):
        high, low = halves(pieces)
        return jnp.concatenate(high + low + high, 1).astype(BF16)

    for layer in range(wf.shape[0]):
        for dx in range(3):
            wf[layer, pl.ds(dx * channels, channels), :] = wide([w[layer, tap(dy), dx] for dy in range(3)])
    for layer in range(wb.shape[0]):
        for dx in range(3):
            pieces = [w[layer, tap(2 - dy), 2 - dx].T for dy in range(3)]
            wb[layer, pl.ds(dx * channels, channels), :] = wide(pieces)
    zeros = lambda count: jnp.zeros((count, channels), F32)
    for s in range(2):
        fronts, backs = [], []
        for dy in range(3):
            slots = [
                jnp.concatenate([zeros(4)] * s + [w_first[:, tap(dy), dx, :], zeros(4 - colours)] + [zeros(4)] * (1 - s), 0)
                for dx in range(3)
            ]
            (high,), (low,) = halves([jnp.concatenate(slots, 0)])
            fronts += [high, high]
            backs += [low, jnp.zeros_like(low)]
        w1[pl.ds(s * channels, channels), :] = jnp.concatenate(fronts + backs, 0).T.astype(BF16)
    last = [
        jnp.concatenate(
            sum([[w_first[:, tap(2 - dy), 2 - dx, :], zeros(8 - colours)] for dx in range(3)], []), 0
        )
        for dy in range(3)
    ]
    w1t[...] = wide(last)


def pack_kernel(rows):
    def kernel(side_ref, fractions, image, baseline, target, x_own, send, tile, sem):
        side = side_ref[0]
        channels = target.shape[0]
        start = pl.multiple_of((1 - side) * (rows - 8), 8)
        fetch = pltpu.make_async_copy(target.at[:, pl.ds(start, 8), :], tile, sem)
        fetch.start()
        base, difference = baseline[...], image[...] - baseline[...]
        colours = base.shape[0]
        zero = jnp.zeros((4 - colours,) + base.shape[1:], F32)
        for s in range(2):
            x_own[pl.ds(4 * s, colours)] = base + fractions[s] * difference
            x_own[pl.ds(4 * s + colours, 4 - colours)] = zero
        for j in range(HALO_X):
            row = jnp.where(side == 0, rows - HALO_X + j, HALO_X - 1 - j)
            send[pl.ds(HALO_T * channels + 8 * j, 8), :] = x_own[:, row, :]
        fetch.wait()
        for j in range(HALO_T):
            row = jnp.where(side == 0, 8 - HALO_T + j, HALO_T - 1 - j)
            send[pl.ds(channels * j, channels), :] = tile[:, row, :]

    return kernel


def spans_of(half):
    near = {"x": (-6, 1), "t": (-4, 3), "a1": (-5, 0), "s1": (-1, 0), "a2": (-4, 1), "s2": (-2, 1)}
    near |= {"d3": (-3, 2), "d2": (-2, 3), "d1": (-1, 4), "out": (0, 5)}
    far = {"x": (0, half + 5), "t": (2, half + 3), "a1": (1, half + 4), "s1": (1, half), "a2": (2, half + 3)}
    far |= {"s2": (2, half + 1), "d3": (3, half + 2), "d2": (4, half + 1), "d1": (5, half), "out": (6, half - 1)}
    return near, far


def far_kernel(rows, half, channels, width):
    def kernel(side_ref, x_own, target, w, w_first, *refs):
        w1, wf, wb, w1t, out = refs[:5]
        edges, (e1, e2) = refs[5:15], refs[15:17]
        xs, s1, s2 = refs[17:20]
        work = refs[20:]
        side = side_ref[0]
        row_of = lambda local: jnp.where(side == 0, local, rows - 1 - local)
        prepare(side, w, w_first, w1, wf, wb, w1t, channels, x_colours(w_first))
        spans = spans_of(half)[1]
        maps = [Maps(work[2 * i : 2 * i + 2], b) for i, b in enumerate((1, 2, 2, 3, 4, 5))]

        def emit(j, value):
            out[j - spans["out"][0]] = value

        run(
            spans, (w1, wf, wb, w1t), xs, 0, maps, (s1, 1, s2, 2),
            lambda j: x_own[:, row_of(j), :], lambda j: target[:, row_of(j), :],
            lambda value, j: value, emit, channels, width,
        )
        a1, a2, _, d3, d2, d1 = maps
        for i, (m, row) in enumerate(((a1, 1), (a2, 2), (d3, 3), (d2, 4), (d1, 5))):
            m.copy(edges[2 * i : 2 * i + 2], row, 2)
        e1[...] = s1[:, 0:4]
        e2[...] = s2[:, 0:2]

    return kernel


def x_colours(w_first):
    return w_first.shape[0]


def near_kernel(rows, half, channels, width):
    def kernel(info, x_own, target, halo, *refs):
        w1, wf, wb, w1t, far_out = refs[:5]
        edges, (e1, e2) = refs[5:15], refs[15:17]
        out = refs[17]
        xs, s1, s2 = refs[18:21]
        work = refs[21:]
        side, exists = info[0], info[1] == 1
        row_of = lambda local: jnp.where(side == 0, local, rows - 1 - local)
        place = lambda local: jnp.where(side == 0, local, half - 1 - local)
        spans = spans_of(half)[0]
        maps = [Maps(work[2 * i : 2 * i + 2], b) for i, b in enumerate((-5, -4, -4, -3, -2, -1))]
        a1, a2, _, d3, d2, d1 = maps
        for i, (m, row) in enumerate(((a1, 1), (a2, 2), (d3, 3), (d2, 4), (d1, 5))):
            m.load(edges[2 * i : 2 * i + 2], row, 2)
        s1[:, 2:6] = e1[...]
        s2[:, 4:6] = e2[...]
        for j in range(6, half):
            out[place(j)] = far_out[j - 6]

        def x_row(j):
            if j < 0:
                return halo[pl.ds(HALO_T * channels + 8 * (j + HALO_X), 8), :]
            return x_own[:, row_of(j), :]

        def t_row(j):
            if j < 0:
                return halo[pl.ds(channels * (j + HALO_T), channels), :]
            return target[:, row_of(j), :]

        def keep(value, j):
            return jnp.where(exists, value, 0.0) if j < 0 else value

        def emit(j, value):
            out[place(j)] = value

        run(
            spans, (w1, wf, wb, w1t), xs, -6, maps, (s1, -1, s2, -2),
            x_row, t_row, keep, emit, channels, width,
        )

    return kernel


def body(image, baseline, w_first, w_rest, target):
    colours, rows, width = image.shape
    channels = target.shape[0]
    half = rows // 2
    space_n, step_n = lax.axis_size("space"), lax.axis_size("step")
    space, step = lax.axis_index("space"), lax.axis_index("step")
    side, group = step % 2, step // 2
    first = (group * 2).astype(F32) + 0.5
    fractions = jnp.stack([first / step_n, (first + 1.0) / step_n])
    exists = jnp.where(side == 0, space > 0, space < space_n - 1)
    info = jnp.stack([side, exists.astype(jnp.int32)]).astype(jnp.int32)
    params = pltpu.CompilerParams(vmem_limit_bytes=40 << 20)
    shape = jax.ShapeDtypeStruct

    x_own, send = pl.pallas_call(
        pack_kernel(rows),
        out_shape=(shape((8, rows, width), F32), shape((HALO_T * channels + HALO_X * 8, width), F32)),
        in_specs=[SMEM, SMEM, VMEM, VMEM, pl.BlockSpec(memory_space=pl.ANY)],
        out_specs=(VMEM, VMEM),
        scratch_shapes=[pltpu.VMEM((channels, 8, width), F32), pltpu.SemaphoreType.DMA(())],
        compiler_params=params,
        name="pack_edges",
    )(info, fractions, image, baseline, target)

    pairs = []
    for i in range(space_n):
        for s in range(step_n):
            source = i + 1 if s % 2 else i - 1
            if 0 <= source < space_n:
                pairs.append((source * step_n + s, i * step_n + s))
    halo = lax.ppermute(send, ("space", "step"), pairs)

    n = 3 * channels
    weight_shapes = [
        shape((2 * channels, 288), BF16),
        shape((2, n, 3 * n), BF16),
        shape((3, n, 3 * n), BF16),
        shape((24, 3 * n), BF16),
    ]
    edge_shapes = [shape((2, 2, channels, width), BF16)] * 10
    edge_shapes += [shape((2, 4, channels, width), F32), shape((2, 2, channels, width), F32)]

    def scratch(x_rows, s1_rows, s2_rows, counts):
        refs = [pltpu.VMEM((x_rows, 48, width), BF16)]
        refs += [pltpu.VMEM((2, r, channels, width), F32) for r in (s1_rows, s2_rows)]
        for i, count in enumerate(counts):
            refs += [pltpu.VMEM((1 if i == 2 else 2, count, channels, width), BF16)] * 2
        return refs

    far = pl.pallas_call(
        far_kernel(rows, half, channels, width),
        out_shape=(*weight_shapes, shape((half - 6, 8, width), F32), *edge_shapes),
        in_specs=[SMEM] + [VMEM] * 4,
        out_specs=(VMEM,) * 17,
        scratch_shapes=scratch(half + 6, half, half, (half + 4, half + 2, half + 2, half, half - 2, half - 4)),
        compiler_params=params,
        name="far_rows",
    )(info, x_own, target, w_rest.transpose(0, 3, 4, 1, 2), w_first.transpose(1, 2, 3, 0))

    y = pl.pallas_call(
        near_kernel(rows, half, channels, width),
        out_shape=shape((half, 8, width), F32),
        in_specs=[SMEM] + [VMEM] * 20,
        out_specs=VMEM,
        scratch_shapes=scratch(8, 6, 6, (8,) * 6),
        compiler_params=params,
        name="near_rows",
    )(info, x_own, target, halo, *far)
    y = y.transpose(1, 0, 2)[:colours]

    def partner(k):
        return lax.ppermute(y, "step", [(i, i ^ k) for i in range(step_n)])

    difference = image - baseline
    if step_n == 4:
        mine, theirs = y + partner(2), partner(1) + partner(3)
        whole = jnp.where(side == 0, jnp.concatenate([mine, theirs], 1), jnp.concatenate([theirs, mine], 1))
    else:
        order = lax.broadcasted_iota(jnp.int32, (2, 1, 1, 1), 0)
        halves = lax.psum(jnp.where(order == side, y[None], 0.0), "step")
        whole = jnp.concatenate([halves[0], halves[1]], 1)
    return difference * whole / step_n


def solution(mesh):
    in_specs = (P(None, "space", None), P(None, "space", None), P(), P(), P(None, "space", None))
    out_specs = P(None, "space", None)
    return jax.shard_map(body, mesh=mesh, in_specs=in_specs, out_specs=out_specs, check_vma=False)
```

```python
import jax
import jax.numpy as jnp
from jax import lax
from jax.experimental import pallas as pl
from jax.experimental.pallas import tpu as pltpu
from jax.sharding import PartitionSpec as P

F32, BF16 = jnp.float32, jnp.bfloat16
HALO_X, HALO_T = 6, 4
VMEM = pl.BlockSpec(memory_space=pltpu.VMEM)
HBM = pl.BlockSpec(memory_space=pltpu.HBM)
SMEM = pl.BlockSpec(memory_space=pltpu.SMEM)


def dot(a, b):
    return jnp.dot(a, b, preferred_element_type=F32)


def split(value):
    high = value.astype(BF16)
    return high, (value - high.astype(F32)).astype(BF16)


def shift_cols(value, by):
    width = value.shape[-1]
    col = lax.broadcasted_iota(jnp.int32, value.shape, value.ndim - 1)
    edge = 0 if by > 0 else width - 1
    return jnp.where(col == edge, 0.0, pltpu.roll(value, by % width, value.ndim - 1))


def combine(y, rows):
    return y[rows : 2 * rows] + shift_cols(y[:rows], 1) + shift_cols(y[2 * rows : 3 * rows], -1)


def silu_and_slope(pre):
    sig = 1.0 / (1.0 + jnp.exp(-pre))
    act = pre * sig
    return act, sig + act * (1.0 - sig)


def conv_row(weights, high, low, index):
    stack = lambda ref: ref[index : index + 3].reshape(3 * ref.shape[1], ref.shape[2])
    upper, lower = stack(high), stack(low)
    return dot(weights, jnp.concatenate([upper, upper, lower], 0))


class Maps:
    def __init__(self, refs, base):
        self.high, self.low = refs
        self.base = base

    def put(self, step, row, value):
        self.high[step, row - self.base], self.low[step, row - self.base] = split(value)

    def conv(self, weights, step, row):
        return conv_row(weights, self.high.at[step], self.low.at[step], row - 1 - self.base)

    def copy(self, refs, row, count):
        for part, ref in zip((self.high, self.low), refs):
            ref[...] = part[:, row - self.base : row - self.base + count]

    def load(self, refs, row, count):
        for part, ref in zip((self.high, self.low), refs):
            part[:, row - self.base : row - self.base + count] = ref[...]


def run(spans, weights, xs, x_base, maps, slopes, x_row, t_row, keep, emit, channels, width):
    w1, wf, wb, w1t = weights
    a1, a2, t, d3, d2, d1 = maps
    s1, s1_base, s2, s2_base = slopes
    rows = lambda name: range(spans[name][0], spans[name][1] + 1)
    inside = lambda name, row: spans[name][0] <= row <= spans[name][1]
    for j in rows("x"):
        x = x_row(j)
        taps = jnp.concatenate([shift_cols(x, 1), x, shift_cols(x, -1)], 0)
        high = taps.astype(BF16).astype(F32)
        xs[j - x_base] = jnp.concatenate([high, taps - high], 0).astype(BF16)
    for j in rows("a1"):
        stack = xs[j - 1 - x_base : j + 2 - x_base].reshape(3 * xs.shape[1], width)
        pre = dot(w1[...], jnp.concatenate([stack, stack], 0))
        for s in range(2):
            act, slope = silu_and_slope(pre[s * channels : (s + 1) * channels])
            a1.put(s, j, keep(act, j))
            if inside("s1", j):
                s1[s, j - s1_base] = keep(slope, j)
    for j in rows("a2"):
        for s in range(2):
            act, slope = silu_and_slope(combine(a1.conv(wf[0], s, j), channels))
            a2.put(s, j, keep(act, j))
            if inside("s2", j):
                s2[s, j - s2_base] = keep(slope, j)
    for j in rows("t"):
        t.put(0, j, t_row(j))
    for j in rows("d3"):
        grad = combine(t.conv(wb[2], 0, j), channels)
        for s in range(2):
            _, slope = silu_and_slope(combine(a2.conv(wf[1], s, j), channels))
            d3.put(s, j, keep(grad * slope, j))
    for j in rows("d2"):
        for s in range(2):
            d2.put(s, j, combine(d3.conv(wb[1], s, j), channels) * s2[s, j - s2_base])
    for j in rows("d1"):
        for s in range(2):
            d1.put(s, j, combine(d2.conv(wb[0], s, j), channels) * s1[s, j - s1_base])
    for j in rows("out"):
        emit(j, combine(d1.conv(w1t[...], 0, j) + d1.conv(w1t[...], 1, j), 8))


def prepare(side, w, w_first, w1, wf, wb, w1t, channels, colours):
    tap = lambda dy: jnp.where(side == 1, 2 - dy, dy)

    def halves(pieces):
        high = [p.astype(BF16).astype(F32) for p in pieces]
        return high, [p - h for p, h in zip(pieces, high)]

    def wide(pieces):
        high, low = halves(pieces)
        return jnp.concatenate(high + low + high, 1).astype(BF16)

    for layer in range(wf.shape[0]):
        for dx in range(3):
            wf[layer, pl.ds(dx * channels, channels), :] = wide([w[layer, tap(dy), dx] for dy in range(3)])
    for layer in range(wb.shape[0]):
        for dx in range(3):
            pieces = [w[layer, tap(2 - dy), 2 - dx].T for dy in range(3)]
            wb[layer, pl.ds(dx * channels, channels), :] = wide(pieces)
    zeros = lambda count: jnp.zeros((count, channels), F32)
    for s in range(2):
        fronts, backs = [], []
        for dy in range(3):
            slots = [
                jnp.concatenate([zeros(4)] * s + [w_first[:, tap(dy), dx, :], zeros(4 - colours)] + [zeros(4)] * (1 - s), 0)
                for dx in range(3)
            ]
            (high,), (low,) = halves([jnp.concatenate(slots, 0)])
            fronts += [high, high]
            backs += [low, jnp.zeros_like(low)]
        w1[pl.ds(s * channels, channels), :] = jnp.concatenate(fronts + backs, 0).T.astype(BF16)
    last = [
        jnp.concatenate(
            sum([[w_first[:, tap(2 - dy), 2 - dx, :], zeros(8 - colours)] for dx in range(3)], []), 0
        )
        for dy in range(3)
    ]
    w1t[...] = wide(last)


def pack_kernel(rows):
    def kernel(side_ref, fractions, image, baseline, target, x_own, send, image_copy, base_copy, sems, row_sems):
        side = side_ref[0]
        channels = target.shape[0]
        copies = []
        for source, landing, i in ((image, image_copy, 0), (baseline, base_copy, 1)):
            copies.append(pltpu.make_async_copy(source, landing, sems.at[i]))
            copies[-1].start()
        for j in range(HALO_T):
            row = jnp.where(side == 0, rows - HALO_T + j, HALO_T - 1 - j)
            place = send.at[pl.ds(channels * j, channels), :]
            copies.append(pltpu.make_async_copy(target.at[:, row, :], place, row_sems.at[j]))
            copies[-1].start()
        copies[0].wait()
        copies[1].wait()
        base, difference = base_copy[...], image_copy[...] - base_copy[...]
        colours = base.shape[0]
        zero = jnp.zeros((4 - colours,) + base.shape[1:], F32)
        for s in range(2):
            x_own[pl.ds(4 * s, colours)] = base + fractions[s] * difference
            x_own[pl.ds(4 * s + colours, 4 - colours)] = zero
        for j in range(HALO_X):
            row = jnp.where(side == 0, rows - HALO_X + j, HALO_X - 1 - j)
            send[pl.ds(HALO_T * channels + 8 * j, 8), :] = x_own[:, row, :]
        for copy in copies[2:]:
            copy.wait()

    return kernel


def spans_of(half):
    near = {"x": (-6, 1), "t": (-4, 3), "a1": (-5, 0), "s1": (-1, 0), "a2": (-4, 1), "s2": (-2, 1)}
    near |= {"d3": (-3, 2), "d2": (-2, 3), "d1": (-1, 4), "out": (0, 5)}
    far = {"x": (0, half + 5), "t": (2, half + 3), "a1": (1, half + 4), "s1": (1, half), "a2": (2, half + 3)}
    far |= {"s2": (2, half + 1), "d3": (3, half + 2), "d2": (4, half + 1), "d1": (5, half), "out": (6, half - 1)}
    return near, far


def fetch_rows(target, landing, sems, row_of, span):
    copies = {}
    for i, local in enumerate(range(span[0], span[1] + 1)):
        copies[local] = pltpu.make_async_copy(target.at[:, row_of(local), :], landing.at[i], sems.at[i])
        copies[local].start()

    def t_row(local):
        copies[local].wait()
        return landing[local - span[0]]

    return t_row


def far_kernel(rows, half, channels, width):
    def kernel(side_ref, x_own, target, w, w_first, *refs):
        w1, wf, wb, w1t, out = refs[:5]
        edges, (e1, e2) = refs[5:15], refs[15:17]
        xs, s1, s2 = refs[17:20]
        w_copy, t_rows, w_sem, t_sems = refs[20:24]
        work = refs[24:]
        side = side_ref[0]
        row_of = lambda local: jnp.where(side == 0, local, rows - 1 - local)
        w_fetch = pltpu.make_async_copy(w, w_copy, w_sem)
        w_fetch.start()
        t_row = fetch_rows(target, t_rows, t_sems, row_of, spans_of(half)[1]["t"])
        w_fetch.wait()
        prepare(side, w_copy, w_first, w1, wf, wb, w1t, channels, x_colours(w_first))
        spans = spans_of(half)[1]
        maps = [Maps(work[2 * i : 2 * i + 2], b) for i, b in enumerate((1, 2, 2, 3, 4, 5))]

        def emit(j, value):
            out[j - spans["out"][0]] = value

        run(
            spans, (w1, wf, wb, w1t), xs, 0, maps, (s1, 1, s2, 2),
            lambda j: x_own[:, row_of(j), :], t_row,
            lambda value, j: value, emit, channels, width,
        )
        a1, a2, _, d3, d2, d1 = maps
        for i, (m, row) in enumerate(((a1, 1), (a2, 2), (d3, 3), (d2, 4), (d1, 5))):
            m.copy(edges[2 * i : 2 * i + 2], row, 2)
        e1[...] = s1[:, 0:4]
        e2[...] = s2[:, 0:2]

    return kernel


def x_colours(w_first):
    return w_first.shape[0]


def near_kernel(rows, half, channels, width):
    def kernel(info, x_own, target, halo, *refs):
        w1, wf, wb, w1t, far_out = refs[:5]
        edges, (e1, e2) = refs[5:15], refs[15:17]
        out = refs[17]
        xs, s1, s2 = refs[18:21]
        t_rows, t_sems = refs[21:23]
        work = refs[23:]
        side, exists = info[0], info[1] == 1
        row_of = lambda local: jnp.where(side == 0, local, rows - 1 - local)
        place = lambda local: jnp.where(side == 0, local, half - 1 - local)
        own_t_row = fetch_rows(target, t_rows, t_sems, row_of, (0, spans_of(half)[0]["t"][1]))
        spans = spans_of(half)[0]
        maps = [Maps(work[2 * i : 2 * i + 2], b) for i, b in enumerate((-5, -4, -4, -3, -2, -1))]
        a1, a2, _, d3, d2, d1 = maps
        for i, (m, row) in enumerate(((a1, 1), (a2, 2), (d3, 3), (d2, 4), (d1, 5))):
            m.load(edges[2 * i : 2 * i + 2], row, 2)
        s1[:, 2:6] = e1[...]
        s2[:, 4:6] = e2[...]
        for j in range(6, half):
            out[place(j)] = far_out[j - 6]

        def x_row(j):
            if j < 0:
                return halo[pl.ds(HALO_T * channels + 8 * (j + HALO_X), 8), :]
            return x_own[:, row_of(j), :]

        def t_row(j):
            if j < 0:
                return halo[pl.ds(channels * (j + HALO_T), channels), :]
            return own_t_row(j)

        def keep(value, j):
            return jnp.where(exists, value, 0.0) if j < 0 else value

        def emit(j, value):
            out[place(j)] = value

        run(
            spans, (w1, wf, wb, w1t), xs, -6, maps, (s1, -1, s2, -2),
            x_row, t_row, keep, emit, channels, width,
        )

    return kernel


def body(image, baseline, w_first, w_rest, target):
    colours, rows, width = image.shape
    channels = target.shape[0]
    half = rows // 2
    space_n, step_n = lax.axis_size("space"), lax.axis_size("step")
    space, step = lax.axis_index("space"), lax.axis_index("step")
    side, group = step % 2, step // 2
    first = (group * 2).astype(F32) + 0.5
    fractions = jnp.stack([first / step_n, (first + 1.0) / step_n])
    exists = jnp.where(side == 0, space > 0, space < space_n - 1)
    info = jnp.stack([side, exists.astype(jnp.int32)]).astype(jnp.int32)
    in_hbm = lambda array: pltpu.with_memory_space_constraint(array, pltpu.HBM)
    target_hbm = in_hbm(target)
    w_hbm = in_hbm(w_rest.transpose(0, 3, 4, 1, 2))
    params = pltpu.CompilerParams(vmem_limit_bytes=40 << 20)
    shape = jax.ShapeDtypeStruct

    x_own, send = pl.pallas_call(
        pack_kernel(rows),
        out_shape=(shape((8, rows, width), F32), shape((HALO_T * channels + HALO_X * 8, width), F32)),
        in_specs=[SMEM, SMEM, HBM, HBM, HBM],
        out_specs=(VMEM, VMEM),
        scratch_shapes=[pltpu.VMEM((colours, rows, width), F32)] * 2
        + [pltpu.SemaphoreType.DMA((2,)), pltpu.SemaphoreType.DMA((HALO_T,))],
        compiler_params=params,
        name="pack_edges",
    )(info, fractions, in_hbm(image), in_hbm(baseline), target_hbm)

    pairs = []
    for i in range(space_n):
        for s in range(step_n):
            source = i + 1 if s % 2 else i - 1
            if 0 <= source < space_n:
                pairs.append((source * step_n + s, i * step_n + s))
    halo = lax.ppermute(send, ("space", "step"), pairs)

    n = 3 * channels
    weight_shapes = [
        shape((2 * channels, 288), BF16),
        shape((2, n, 3 * n), BF16),
        shape((3, n, 3 * n), BF16),
        shape((24, 3 * n), BF16),
    ]
    edge_shapes = [shape((2, 2, channels, width), BF16)] * 10
    edge_shapes += [shape((2, 4, channels, width), F32), shape((2, 2, channels, width), F32)]

    def scratch(x_rows, s1_rows, s2_rows, t_rows, counts, weights=False):
        refs = [pltpu.VMEM((x_rows, 48, width), BF16)]
        refs += [pltpu.VMEM((2, r, channels, width), F32) for r in (s1_rows, s2_rows)]
        refs += [pltpu.VMEM((3, 3, 3, channels, channels), F32)] * weights
        refs += [pltpu.VMEM((t_rows, channels, width), F32)]
        refs += [pltpu.SemaphoreType.DMA(())] * weights + [pltpu.SemaphoreType.DMA((t_rows,))]
        for i, count in enumerate(counts):
            refs += [pltpu.VMEM((1 if i == 2 else 2, count, channels, width), BF16)] * 2
        return refs

    far = pl.pallas_call(
        far_kernel(rows, half, channels, width),
        out_shape=(*weight_shapes, shape((half - 6, 8, width), F32), *edge_shapes),
        in_specs=[SMEM, VMEM, HBM, HBM, VMEM],
        out_specs=(VMEM,) * 17,
        scratch_shapes=scratch(half + 6, half, half, half + 2, (half + 4, half + 2, half + 2, half, half - 2, half - 4), True),
        compiler_params=params,
        name="far_rows",
    )(info, x_own, target_hbm, w_hbm, w_first.transpose(1, 2, 3, 0))

    y = pl.pallas_call(
        near_kernel(rows, half, channels, width),
        out_shape=shape((half, 8, width), F32),
        in_specs=[SMEM, VMEM, HBM] + [VMEM] * 18,
        out_specs=VMEM,
        scratch_shapes=scratch(8, 6, 6, 4, (8,) * 6),
        compiler_params=params,
        name="near_rows",
    )(info, x_own, target_hbm, halo, *far)
    y = y.transpose(1, 0, 2)[:colours]

    def partner(k):
        return lax.ppermute(y, "step", [(i, i ^ k) for i in range(step_n)])

    difference = image - baseline
    if step_n == 4:
        mine, theirs = y + partner(2), partner(1) + partner(3)
        whole = jnp.where(side == 0, jnp.concatenate([mine, theirs], 1), jnp.concatenate([theirs, mine], 1))
    else:
        order = lax.broadcasted_iota(jnp.int32, (2, 1, 1, 1), 0)
        halves = lax.psum(jnp.where(order == side, y[None], 0.0), "step")
        whole = jnp.concatenate([halves[0], halves[1]], 1)
    return difference * whole / step_n


def solution(mesh):
    in_specs = (P(None, "space", None), P(None, "space", None), P(), P(), P(None, "space", None))
    out_specs = P(None, "space", None)
    return jax.shard_map(body, mesh=mesh, in_specs=in_specs, out_specs=out_specs, check_vma=False)
```

```python
import jax
import jax.numpy as jnp
from jax import lax
from jax.experimental import pallas as pl
from jax.experimental.pallas import tpu as pltpu
from jax.sharding import PartitionSpec as P

F32, BF16 = jnp.float32, jnp.bfloat16
HALO_X, HALO_T = 6, 4
VMEM = pl.BlockSpec(memory_space=pltpu.VMEM)
HBM = pl.BlockSpec(memory_space=pltpu.HBM)
SMEM = pl.BlockSpec(memory_space=pltpu.SMEM)


def dot(a, b):
    return jnp.dot(a, b, preferred_element_type=F32)


def split(value):
    high = value.astype(BF16)
    return high, (value - high.astype(F32)).astype(BF16)


def shift_cols(value, by):
    width = value.shape[-1]
    col = lax.broadcasted_iota(jnp.int32, value.shape, value.ndim - 1)
    edge = 0 if by > 0 else width - 1
    return jnp.where(col == edge, 0.0, pltpu.roll(value, by % width, value.ndim - 1))


def combine(y, rows):
    return y[rows : 2 * rows] + shift_cols(y[:rows], 1) + shift_cols(y[2 * rows : 3 * rows], -1)


def silu_and_slope(pre):
    sig = 1.0 / (1.0 + jnp.exp(-pre))
    act = pre * sig
    return act, sig + act * (1.0 - sig)


def conv_row(weights, high, low, index):
    stack = lambda ref: ref[index : index + 3].reshape(3 * ref.shape[1], ref.shape[2])
    upper, lower = stack(high), stack(low)
    return dot(weights, jnp.concatenate([upper, upper, lower], 0))


class Maps:
    def __init__(self, refs, base):
        self.high, self.low = refs
        self.base = base

    def put(self, step, row, value):
        self.high[step, row - self.base], self.low[step, row - self.base] = split(value)

    def conv(self, weights, step, row):
        return conv_row(weights, self.high.at[step], self.low.at[step], row - 1 - self.base)

    def copy(self, refs, row, count):
        for part, ref in zip((self.high, self.low), refs):
            ref[...] = part[:, row - self.base : row - self.base + count]

    def load(self, refs, row, count):
        for part, ref in zip((self.high, self.low), refs):
            part[:, row - self.base : row - self.base + count] = ref[...]


def run(spans, weights, xs, x_base, maps, slopes, x_row, t_row, keep, emit, channels, width, ready=lambda: None):
    w1, wf, wb, w1t = weights
    a1, a2, t, d3, d2, d1 = maps
    s1, s1_base, s2, s2_base = slopes
    rows = lambda name: range(spans[name][0], spans[name][1] + 1)
    inside = lambda name, row: spans[name][0] <= row <= spans[name][1]
    for j in rows("x"):
        x = x_row(j)
        taps = jnp.concatenate([shift_cols(x, 1), x, shift_cols(x, -1)], 0)
        high = taps.astype(BF16).astype(F32)
        xs[j - x_base] = jnp.concatenate([high, taps - high], 0).astype(BF16)
    for j in rows("a1"):
        stack = xs[j - 1 - x_base : j + 2 - x_base].reshape(3 * xs.shape[1], width)
        pre = dot(w1[...], jnp.concatenate([stack, stack], 0))
        for s in range(2):
            act, slope = silu_and_slope(pre[s * channels : (s + 1) * channels])
            a1.put(s, j, keep(act, j))
            if inside("s1", j):
                s1[s, j - s1_base] = keep(slope, j)
    ready()
    for j in rows("a2"):
        for s in range(2):
            act, slope = silu_and_slope(combine(a1.conv(wf[0], s, j), channels))
            a2.put(s, j, keep(act, j))
            if inside("s2", j):
                s2[s, j - s2_base] = keep(slope, j)
    for j in rows("t"):
        t.put(0, j, t_row(j))
    for j in rows("d3"):
        grad = combine(t.conv(wb[2], 0, j), channels)
        for s in range(2):
            _, slope = silu_and_slope(combine(a2.conv(wf[1], s, j), channels))
            d3.put(s, j, keep(grad * slope, j))
    for j in rows("d2"):
        for s in range(2):
            d2.put(s, j, combine(d3.conv(wb[1], s, j), channels) * s2[s, j - s2_base])
    for j in rows("d1"):
        for s in range(2):
            d1.put(s, j, combine(d2.conv(wb[0], s, j), channels) * s1[s, j - s1_base])
    for j in rows("out"):
        emit(j, combine(d1.conv(w1t[...], 0, j) + d1.conv(w1t[...], 1, j), 8))


def halves(pieces):
    high = [p.astype(BF16).astype(F32) for p in pieces]
    return high, [p - h for p, h in zip(pieces, high)]


def wide(pieces):
    high, low = halves(pieces)
    return jnp.concatenate(high + low + high, 1).astype(BF16)


def prepare_rest(side, w, wf, wb, channels):
    tap = lambda dy: jnp.where(side == 1, 2 - dy, dy)

    for layer in range(wf.shape[0]):
        for dx in range(3):
            wf[layer, pl.ds(dx * channels, channels), :] = wide([w[layer, tap(dy), dx] for dy in range(3)])
    for layer in range(wb.shape[0]):
        for dx in range(3):
            pieces = [w[layer, tap(2 - dy), 2 - dx].T for dy in range(3)]
            wb[layer, pl.ds(dx * channels, channels), :] = wide(pieces)


def prepare_first(side, w_first, w1, w1t, channels, colours):
    tap = lambda dy: jnp.where(side == 1, 2 - dy, dy)
    zeros = lambda count: jnp.zeros((count, channels), F32)
    for s in range(2):
        fronts, backs = [], []
        for dy in range(3):
            slots = [
                jnp.concatenate([zeros(4)] * s + [w_first[:, tap(dy), dx, :], zeros(4 - colours)] + [zeros(4)] * (1 - s), 0)
                for dx in range(3)
            ]
            (high,), (low,) = halves([jnp.concatenate(slots, 0)])
            fronts += [high, high]
            backs += [low, jnp.zeros_like(low)]
        w1[pl.ds(s * channels, channels), :] = jnp.concatenate(fronts + backs, 0).T.astype(BF16)
    last = [
        jnp.concatenate(
            sum([[w_first[:, tap(2 - dy), 2 - dx, :], zeros(8 - colours)] for dx in range(3)], []), 0
        )
        for dy in range(3)
    ]
    w1t[...] = wide(last)


def pack_kernel(rows):
    def kernel(side_ref, fractions, image, baseline, target, x_own, send, image_copy, base_copy, sems, row_sems):
        side = side_ref[0]
        channels = target.shape[0]
        copies = []
        for source, landing, i in ((image, image_copy, 0), (baseline, base_copy, 1)):
            copies.append(pltpu.make_async_copy(source, landing, sems.at[i]))
            copies[-1].start()
        for j in range(HALO_T):
            row = jnp.where(side == 0, rows - HALO_T + j, HALO_T - 1 - j)
            place = send.at[pl.ds(channels * j, channels), :]
            copies.append(pltpu.make_async_copy(target.at[:, row, :], place, row_sems.at[j]))
            copies[-1].start()
        copies[0].wait()
        copies[1].wait()
        base, difference = base_copy[...], image_copy[...] - base_copy[...]
        colours = base.shape[0]
        zero = jnp.zeros((4 - colours,) + base.shape[1:], F32)
        for s in range(2):
            x_own[pl.ds(4 * s, colours)] = base + fractions[s] * difference
            x_own[pl.ds(4 * s + colours, 4 - colours)] = zero
        for j in range(HALO_X):
            row = jnp.where(side == 0, rows - HALO_X + j, HALO_X - 1 - j)
            send[pl.ds(HALO_T * channels + 8 * j, 8), :] = x_own[:, row, :]
        for copy in copies[2:]:
            copy.wait()

    return kernel


def spans_of(half):
    near = {"x": (-6, 1), "t": (-4, 3), "a1": (-5, 0), "s1": (-1, 0), "a2": (-4, 1), "s2": (-2, 1)}
    near |= {"d3": (-3, 2), "d2": (-2, 3), "d1": (-1, 4), "out": (0, 5)}
    far = {"x": (0, half + 5), "t": (2, half + 3), "a1": (1, half + 4), "s1": (1, half), "a2": (2, half + 3)}
    far |= {"s2": (2, half + 1), "d3": (3, half + 2), "d2": (4, half + 1), "d1": (5, half), "out": (6, half - 1)}
    return near, far


def fetch_rows(target, landing, sems, row_of):
    copies = []
    for local in range(landing.shape[0]):
        copies.append(pltpu.make_async_copy(target.at[:, row_of(local), :], landing.at[local], sems.at[local]))
        copies[-1].start()
    return lambda local: copies[local].wait()


def far_kernel(rows, half, channels, width):
    def kernel(side_ref, x_own, target, w, w_first, *refs):
        w1, wf, wb, w1t, out = refs[:5]
        edges, (e1, e2) = refs[5:15], refs[15:17]
        t_rows = refs[17]
        xs, s1, s2, w_copy, w_sem, t_sems = refs[18:24]
        work = refs[24:]
        side = side_ref[0]
        row_of = lambda local: jnp.where(side == 0, local, rows - 1 - local)
        w_fetch = pltpu.make_async_copy(w, w_copy, w_sem)
        w_fetch.start()
        t_row = fetch_rows(target, t_rows, t_sems, row_of)
        prepare_first(side, w_first, w1, w1t, channels, w_first.shape[0])

        def ready():
            w_fetch.wait()
            prepare_rest(side, w_copy, wf, wb, channels)
            for local in range(t_rows.shape[0]):
                t_row(local)

        spans = spans_of(half)[1]
        maps = [Maps(work[2 * i : 2 * i + 2], b) for i, b in enumerate((1, 2, 2, 3, 4, 5))]

        def emit(j, value):
            out[j - spans["out"][0]] = value

        run(
            spans, (w1, wf, wb, w1t), xs, 0, maps, (s1, 1, s2, 2),
            lambda j: x_own[:, row_of(j), :], lambda j: t_rows[j],
            lambda value, j: value, emit, channels, width, ready,
        )
        a1, a2, _, d3, d2, d1 = maps
        for i, (m, row) in enumerate(((a1, 1), (a2, 2), (d3, 3), (d2, 4), (d1, 5))):
            m.copy(edges[2 * i : 2 * i + 2], row, 2)
        e1[...] = s1[:, 0:4]
        e2[...] = s2[:, 0:2]

    return kernel


def near_kernel(rows, half, channels, width):
    def kernel(info, x_own, halo, *refs):
        w1, wf, wb, w1t, far_out = refs[:5]
        edges, (e1, e2) = refs[5:15], refs[15:17]
        t_rows, out = refs[17:19]
        xs, s1, s2 = refs[19:22]
        work = refs[22:]
        side, exists = info[0], info[1] == 1
        row_of = lambda local: jnp.where(side == 0, local, rows - 1 - local)
        place = lambda local: jnp.where(side == 0, local, half - 1 - local)
        spans = spans_of(half)[0]
        maps = [Maps(work[2 * i : 2 * i + 2], b) for i, b in enumerate((-5, -4, -4, -3, -2, -1))]
        a1, a2, _, d3, d2, d1 = maps
        for i, (m, row) in enumerate(((a1, 1), (a2, 2), (d3, 3), (d2, 4), (d1, 5))):
            m.load(edges[2 * i : 2 * i + 2], row, 2)
        s1[:, 2:6] = e1[...]
        s2[:, 4:6] = e2[...]
        for j in range(6, half):
            out[place(j)] = far_out[j - 6]

        def x_row(j):
            if j < 0:
                return halo[pl.ds(HALO_T * channels + 8 * (j + HALO_X), 8), :]
            return x_own[:, row_of(j), :]

        def t_row(j):
            if j < 0:
                return halo[pl.ds(channels * (j + HALO_T), channels), :]
            return t_rows[j]

        def keep(value, j):
            return jnp.where(exists, value, 0.0) if j < 0 else value

        def emit(j, value):
            out[place(j)] = value

        run(
            spans, (w1, wf, wb, w1t), xs, -6, maps, (s1, -1, s2, -2),
            x_row, t_row, keep, emit, channels, width,
        )

    return kernel


def body(image, baseline, w_first, w_rest, target):
    colours, rows, width = image.shape
    channels = target.shape[0]
    half = rows // 2
    space_n, step_n = lax.axis_size("space"), lax.axis_size("step")
    space, step = lax.axis_index("space"), lax.axis_index("step")
    side, group = step % 2, step // 2
    first = (group * 2).astype(F32) + 0.5
    fractions = jnp.stack([first / step_n, (first + 1.0) / step_n])
    exists = jnp.where(side == 0, space > 0, space < space_n - 1)
    info = jnp.stack([side, exists.astype(jnp.int32)]).astype(jnp.int32)
    in_hbm = lambda array: pltpu.with_memory_space_constraint(array, pltpu.HBM)
    target_hbm = in_hbm(target)
    w_hbm = in_hbm(w_rest.transpose(0, 3, 4, 1, 2))
    params = pltpu.CompilerParams(vmem_limit_bytes=40 << 20)
    shape = jax.ShapeDtypeStruct

    x_own, send = pl.pallas_call(
        pack_kernel(rows),
        out_shape=(shape((8, rows, width), F32), shape((HALO_T * channels + HALO_X * 8, width), F32)),
        in_specs=[SMEM, SMEM, HBM, HBM, HBM],
        out_specs=(VMEM, VMEM),
        scratch_shapes=[pltpu.VMEM((colours, rows, width), F32)] * 2
        + [pltpu.SemaphoreType.DMA((2,)), pltpu.SemaphoreType.DMA((HALO_T,))],
        compiler_params=params,
        name="pack_edges",
    )(info, fractions, in_hbm(image), in_hbm(baseline), target_hbm)

    pairs = []
    for i in range(space_n):
        for s in range(step_n):
            source = i + 1 if s % 2 else i - 1
            if 0 <= source < space_n:
                pairs.append((source * step_n + s, i * step_n + s))
    halo = lax.ppermute(send, ("space", "step"), pairs)

    n = 3 * channels
    weight_shapes = [
        shape((2 * channels, 288), BF16),
        shape((2, n, 3 * n), BF16),
        shape((3, n, 3 * n), BF16),
        shape((24, 3 * n), BF16),
    ]
    edge_shapes = [shape((2, 2, channels, width), BF16)] * 10
    edge_shapes += [shape((2, 4, channels, width), F32), shape((2, 2, channels, width), F32)]

    def scratch(x_rows, s1_rows, s2_rows, counts, landing=0):
        refs = [pltpu.VMEM((x_rows, 48, width), BF16)]
        refs += [pltpu.VMEM((2, r, channels, width), F32) for r in (s1_rows, s2_rows)]
        if landing:
            refs += [pltpu.VMEM((3, 3, 3, channels, channels), F32)]
            refs += [pltpu.SemaphoreType.DMA(()), pltpu.SemaphoreType.DMA((landing,))]
        for i, count in enumerate(counts):
            refs += [pltpu.VMEM((1 if i == 2 else 2, count, channels, width), BF16)] * 2
        return refs

    far = pl.pallas_call(
        far_kernel(rows, half, channels, width),
        out_shape=(*weight_shapes, shape((half - 6, 8, width), F32), *edge_shapes, shape((half + 4, channels, width), F32)),
        in_specs=[SMEM, VMEM, HBM, HBM, VMEM],
        out_specs=(VMEM,) * 18,
        scratch_shapes=scratch(half + 6, half, half, (half + 4, half + 2, half + 2, half, half - 2, half - 4), half + 4),
        compiler_params=params,
        name="far_rows",
    )(info, x_own, target_hbm, w_hbm, w_first.transpose(1, 2, 3, 0))

    y = pl.pallas_call(
        near_kernel(rows, half, channels, width),
        out_shape=shape((half, 8, width), F32),
        in_specs=[SMEM] + [VMEM] * 20,
        out_specs=VMEM,
        scratch_shapes=scratch(8, 6, 6, (8,) * 6),
        compiler_params=params,
        name="near_rows",
    )(info, x_own, halo, *far)
    y = y.transpose(1, 0, 2)[:colours]

    def partner(k):
        return lax.ppermute(y, "step", [(i, i ^ k) for i in range(step_n)])

    difference = image - baseline
    if step_n == 4:
        mine, theirs = y + partner(2), partner(1) + partner(3)
        whole = jnp.where(side == 0, jnp.concatenate([mine, theirs], 1), jnp.concatenate([theirs, mine], 1))
    else:
        order = lax.broadcasted_iota(jnp.int32, (2, 1, 1, 1), 0)
        halves = lax.psum(jnp.where(order == side, y[None], 0.0), "step")
        whole = jnp.concatenate([halves[0], halves[1]], 1)
    return difference * whole / step_n


def solution(mesh):
    in_specs = (P(None, "space", None), P(None, "space", None), P(), P(), P(None, "space", None))
    out_specs = P(None, "space", None)
    return jax.shard_map(body, mesh=mesh, in_specs=in_specs, out_specs=out_specs, check_vma=False)
```

```python
import jax
import jax.numpy as jnp
from jax import lax
from jax.experimental import pallas as pl
from jax.experimental.pallas import tpu as pltpu
from jax.sharding import PartitionSpec as P

F32, BF16 = jnp.float32, jnp.bfloat16
HALO_X, HALO_T = 6, 4
VMEM = pl.BlockSpec(memory_space=pltpu.VMEM)
HBM = pl.BlockSpec(memory_space=pltpu.HBM)
SMEM = pl.BlockSpec(memory_space=pltpu.SMEM)


def dot(a, b):
    return jnp.dot(a, b, preferred_element_type=F32)


def split(value):
    high = value.astype(BF16)
    return high, (value - high.astype(F32)).astype(BF16)


def shift_cols(value, by):
    width = value.shape[-1]
    rolled = pltpu.roll(value, by % width, 1)
    cut = 128 if by > 0 else width - 128
    left, right = rolled[:, :cut], rolled[:, cut:]
    col = lax.broadcasted_iota(jnp.int32, (value.shape[0], 128), 1)
    if by > 0:
        left = jnp.where(col == 0, 0.0, left)
    else:
        right = jnp.where(col == 127, 0.0, right)
    return jnp.concatenate([left, right], 1)


def combine(y, rows):
    return y[rows : 2 * rows] + shift_cols(y[:rows], 1) + shift_cols(y[2 * rows : 3 * rows], -1)


def silu_and_slope(pre):
    sig = 1.0 / (1.0 + jnp.exp(-pre))
    act = pre * sig
    return act, sig + act * (1.0 - sig)


class Maps:
    def __init__(self, quads, rows_ref, base):
        self.quads, self.rows_ref, self.base = quads, rows_ref, base

    def add(self, step, quad, rows):
        channels = rows[0].shape[0]
        first, second, third, fourth = rows
        sums = (first - third, second + third, third - second, second - fourth)
        for i, value in enumerate(sums):
            high, low = split(value)
            self.quads[step, quad, i, :channels], self.quads[step, quad, i, channels:] = high, low

    def put(self, step, row, value):
        at = row - self.base
        self.rows_ref[step, at] = value
        if at % 2 and at >= 3:
            old = [self.rows_ref[step, at - k] for k in (3, 2, 1)]
            self.add(step, (at - 3) // 2, (*old, value))

    def seal(self, step):
        last = self.rows_ref.shape[1]
        self.add(step, last // 2 - 2, [self.rows_ref[step, last - k] for k in (4, 3, 2, 1)])

    def conv(self, weights, step, row):
        quad = (row - 1 - self.base) // 2
        products = []
        for i in range(4):
            both = self.quads[step, quad, i]
            high, low = both[: both.shape[0] // 2], both[both.shape[0] // 2 :]
            products.append(dot(weights[i], jnp.concatenate([high, high, low], 0)))
        return products[0] + (products[1] + products[2]), (products[1] - products[2]) - products[3]


def run(spans, weights, xs, x_base, maps, slopes, x_row, t_row, keep, emit, channels, width, ready, sealed):
    w1, wf, wb, w1t = weights
    a1, a2, t, d3, d2, d1 = maps
    s1, s1_base, s2, s2_base = slopes
    rows = lambda name: range(spans[name][0], spans[name][1] + 1)
    pairs = lambda name: range(spans[name][0], spans[name][1] + 1, 2)
    inside = lambda name, row: spans[name][0] <= row <= spans[name][1]

    def seal(m):
        if sealed:
            m.seal(0)
            m.seal(1)

    for j in rows("x"):
        x = x_row(j)
        taps = jnp.concatenate([shift_cols(x, 1), x, shift_cols(x, -1)], 0)
        high = taps.astype(BF16).astype(F32)
        xs[j - x_base] = jnp.concatenate([high, taps - high], 0).astype(BF16)
    for j in rows("a1"):
        stack = xs[j - 1 - x_base : j + 2 - x_base].reshape(3 * xs.shape[1], width)
        pre = dot(w1[...], jnp.concatenate([stack, stack], 0))
        for s in range(2):
            act, slope = silu_and_slope(pre[s * channels : (s + 1) * channels])
            a1.put(s, j, keep(act, j))
            if inside("s1", j):
                s1[s, j - s1_base] = keep(slope, j)
    seal(a1)
    ready()
    for i in pairs("a2"):
        for s in range(2):
            for j, y in zip((i, i + 1), a1.conv(wf.at[0], s, i)):
                act, slope = silu_and_slope(combine(y, channels))
                a2.put(s, j, keep(act, j))
                if inside("s2", j):
                    s2[s, j - s2_base] = keep(slope, j)
    seal(a2)
    for j in pairs("t"):
        if j + 3 <= spans["t"][1]:
            t.add(0, (j - t.base) // 2, [t_row(j + k) for k in range(4)])
    for i in pairs("d3"):
        grads = [combine(y, channels) for y in t.conv(wb.at[2], 0, i)]
        for s in range(2):
            for j, grad, y in zip((i, i + 1), grads, a2.conv(wf.at[1], s, i)):
                _, slope = silu_and_slope(combine(y, channels))
                d3.put(s, j, keep(grad * slope, j))
    seal(d3)
    for i in pairs("d2"):
        for s in range(2):
            for j, y in zip((i, i + 1), d3.conv(wb.at[1], s, i)):
                d2.put(s, j, combine(y, channels) * s2[s, j - s2_base])
    seal(d2)
    for i in pairs("d1"):
        for s in range(2):
            for j, y in zip((i, i + 1), d2.conv(wb.at[0], s, i)):
                d1.put(s, j, combine(y, channels) * s1[s, j - s1_base])
    seal(d1)
    for i in pairs("out"):
        zero, one = (d1.conv(w1t, s, i) for s in range(2))
        for j, y, z in zip((i, i + 1), zero, one):
            emit(j, combine(y + z, 8))


def halves(pieces):
    high = [p.astype(BF16).astype(F32) for p in pieces]
    return high, [p - h for p, h in zip(pieces, high)]


def wide(pieces):
    high, low = halves(pieces)
    return jnp.concatenate(high + low + high, 1).astype(BF16)


def filters(taps):
    even, odd = 0.5 * (taps[0] + taps[2]), 0.5 * taps[1]
    return taps[0], even + odd, even - odd, taps[2]


def prepare_rest(side, w, wf, wb, channels):
    tap = lambda dy: jnp.where(side == 1, 2 - dy, dy)
    for dx in range(3):
        place = pl.ds(dx * channels, channels)
        for layer in range(wf.shape[0]):
            for i, piece in enumerate(filters([w[layer, tap(dy), dx] for dy in range(3)])):
                wf[layer, i, place, :] = wide([piece])
        for layer in range(wb.shape[0]):
            for i, piece in enumerate(filters([w[layer, tap(2 - dy), 2 - dx] for dy in range(3)])):
                wb[layer, i, place, :] = wide([piece.T])


def prepare_first(side, w_first, w1, w1t, channels, colours):
    tap = lambda dy: jnp.where(side == 1, 2 - dy, dy)
    zeros = lambda count: jnp.zeros((count, channels), F32)
    for s in range(2):
        fronts, backs = [], []
        for dy in range(3):
            slots = [
                jnp.concatenate([zeros(4)] * s + [w_first[:, tap(dy), dx, :], zeros(4 - colours)] + [zeros(4)] * (1 - s), 0)
                for dx in range(3)
            ]
            (high,), (low,) = halves([jnp.concatenate(slots, 0)])
            fronts += [high, high]
            backs += [low, jnp.zeros_like(low)]
        w1[pl.ds(s * channels, channels), :] = jnp.concatenate(fronts + backs, 0).T.astype(BF16)
    last = [
        jnp.concatenate(
            sum([[w_first[:, tap(2 - dy), 2 - dx, :], zeros(8 - colours)] for dx in range(3)], []), 0
        )
        for dy in range(3)
    ]
    for i, piece in enumerate(filters(last)):
        w1t[i] = wide([piece])


def pack_kernel(rows):
    def kernel(side_ref, fractions, image, baseline, target, x_own, send, image_copy, base_copy, sems, row_sems):
        side = side_ref[0]
        channels = target.shape[0]
        copies = []
        for source, landing, i in ((image, image_copy, 0), (baseline, base_copy, 1)):
            copies.append(pltpu.make_async_copy(source, landing, sems.at[i]))
            copies[-1].start()
        for j in range(HALO_T):
            row = jnp.where(side == 0, rows - HALO_T + j, HALO_T - 1 - j)
            place = send.at[pl.ds(channels * j, channels), :]
            copies.append(pltpu.make_async_copy(target.at[:, row, :], place, row_sems.at[j]))
            copies[-1].start()
        copies[0].wait()
        copies[1].wait()
        base, difference = base_copy[...], image_copy[...] - base_copy[...]
        colours = base.shape[0]
        zero = jnp.zeros((4 - colours,) + base.shape[1:], F32)
        for s in range(2):
            x_own[pl.ds(4 * s, colours)] = base + fractions[s] * difference
            x_own[pl.ds(4 * s + colours, 4 - colours)] = zero
        for j in range(HALO_X):
            row = jnp.where(side == 0, rows - HALO_X + j, HALO_X - 1 - j)
            send[pl.ds(HALO_T * channels + 8 * j, 8), :] = x_own[:, row, :]
        for copy in copies[2:]:
            copy.wait()

    return kernel


def spans_of(half):
    near = {"x": (-6, 1), "t": (-4, 3), "a1": (-5, 0), "s1": (-1, 0), "a2": (-4, 1), "s2": (-2, 1)}
    near |= {"d3": (-3, 2), "d2": (-2, 3), "d1": (-1, 4), "out": (0, 5)}
    far = {"x": (0, half + 5), "t": (2, half + 3), "a1": (1, half + 4), "s1": (1, half), "a2": (2, half + 3)}
    far |= {"s2": (2, half + 1), "d3": (3, half + 2), "d2": (4, half + 1), "d1": (5, half), "out": (6, half - 1)}
    return near, far


def fetch_rows(target, landing, sems, row_of):
    copies = []
    for local in range(landing.shape[0]):
        copies.append(pltpu.make_async_copy(target.at[:, row_of(local), :], landing.at[local], sems.at[local]))
        copies[-1].start()
    return lambda local: copies[local].wait()


def build_maps(work, bases):
    quads, floats = work[:6], list(work[6:])
    floats.insert(2, None)
    return [Maps(q, r, base) for q, r, base in zip(quads, floats, bases)]


def far_kernel(rows, half, channels, width):
    def kernel(side_ref, x_own, target, w, w_first, *refs):
        w1, wf, wb, w1t, out = refs[:5]
        edges, (e1, e2) = refs[5:10], refs[10:12]
        t_rows = refs[12]
        xs, s1, s2, w_copy, w_sem, t_sems = refs[13:19]
        work = refs[19:]
        side = side_ref[0]
        row_of = lambda local: jnp.where(side == 0, local, rows - 1 - local)
        w_fetch = pltpu.make_async_copy(w, w_copy, w_sem)
        w_fetch.start()
        t_row = fetch_rows(target, t_rows, t_sems, row_of)
        prepare_first(side, w_first, w1, w1t, channels, w_first.shape[0])

        def ready():
            w_fetch.wait()
            prepare_rest(side, w_copy, wf, wb, channels)
            for local in range(t_rows.shape[0]):
                t_row(local)

        spans = spans_of(half)[1]
        maps = build_maps(work, (1, 2, 2, 3, 4, 5))

        def emit(j, value):
            out[j - spans["out"][0]] = value

        run(
            spans, (w1, wf, wb, w1t), xs, 0, maps, (s1, 1, s2, 2),
            lambda j: x_own[:, row_of(j), :], lambda j: t_rows[j],
            lambda value, j: value, emit, channels, width, ready, False,
        )
        for m, edge in zip(maps[:2] + maps[3:], edges):
            edge[...] = m.rows_ref[:, 0:2]
        e1[...] = s1[:, 0:4]
        e2[...] = s2[:, 0:2]

    return kernel


def near_kernel(rows, half, channels, width):
    def kernel(info, x_own, halo, *refs):
        w1, wf, wb, w1t, far_out = refs[:5]
        edges, (e1, e2) = refs[5:10], refs[10:12]
        t_rows, out = refs[12:14]
        xs, s1, s2 = refs[14:17]
        work = refs[17:]
        side, exists = info[0], info[1] == 1
        row_of = lambda local: jnp.where(side == 0, local, rows - 1 - local)
        place = lambda local: jnp.where(side == 0, local, half - 1 - local)
        spans = spans_of(half)[0]
        maps = build_maps(work, (-5, -4, -4, -3, -2, -1))
        for m, edge in zip(maps[:2] + maps[3:], edges):
            m.rows_ref[:, 6:8] = edge[...]
        s1[:, 2:6] = e1[...]
        s2[:, 4:6] = e2[...]
        for j in range(6, half):
            out[place(j)] = far_out[j - 6]

        def x_row(j):
            if j < 0:
                return halo[pl.ds(HALO_T * channels + 8 * (j + HALO_X), 8), :]
            return x_own[:, row_of(j), :]

        def t_row(j):
            if j < 0:
                return halo[pl.ds(channels * (j + HALO_T), channels), :]
            return t_rows[j]

        def keep(value, j):
            return jnp.where(exists, value, 0.0) if j < 0 else value

        def emit(j, value):
            out[place(j)] = value

        run(
            spans, (w1, wf, wb, w1t), xs, -6, maps, (s1, -1, s2, -2),
            x_row, t_row, keep, emit, channels, width, lambda: None, True,
        )

    return kernel


def body(image, baseline, w_first, w_rest, target):
    colours, rows, width = image.shape
    channels = target.shape[0]
    half = rows // 2
    space_n, step_n = lax.axis_size("space"), lax.axis_size("step")
    space, step = lax.axis_index("space"), lax.axis_index("step")
    side, group = step % 2, step // 2
    first = (group * 2).astype(F32) + 0.5
    fractions = jnp.stack([first / step_n, (first + 1.0) / step_n])
    exists = jnp.where(side == 0, space > 0, space < space_n - 1)
    info = jnp.stack([side, exists.astype(jnp.int32)]).astype(jnp.int32)
    in_hbm = lambda array: pltpu.with_memory_space_constraint(array, pltpu.HBM)
    target_hbm = in_hbm(target)
    w_hbm = in_hbm(w_rest.transpose(0, 3, 4, 1, 2))
    params = pltpu.CompilerParams(vmem_limit_bytes=40 << 20)
    shape = jax.ShapeDtypeStruct

    x_own, send = pl.pallas_call(
        pack_kernel(rows),
        out_shape=(shape((8, rows, width), F32), shape((HALO_T * channels + HALO_X * 8, width), F32)),
        in_specs=[SMEM, SMEM, HBM, HBM, HBM],
        out_specs=(VMEM, VMEM),
        scratch_shapes=[pltpu.VMEM((colours, rows, width), F32)] * 2
        + [pltpu.SemaphoreType.DMA((2,)), pltpu.SemaphoreType.DMA((HALO_T,))],
        compiler_params=params,
        name="pack_edges",
    )(info, fractions, in_hbm(image), in_hbm(baseline), target_hbm)

    pairs = []
    for i in range(space_n):
        for s in range(step_n):
            source = i + 1 if s % 2 else i - 1
            if 0 <= source < space_n:
                pairs.append((source * step_n + s, i * step_n + s))
    halo = lax.ppermute(send, ("space", "step"), pairs)

    n = 3 * channels
    weight_shapes = [
        shape((2 * channels, 288), BF16),
        shape((2, 4, n, n), BF16),
        shape((3, 4, n, n), BF16),
        shape((4, 24, n), BF16),
    ]
    edge_shapes = [shape((2, 2, channels, width), F32)] * 5
    edge_shapes += [shape((2, 4, channels, width), F32), shape((2, 2, channels, width), F32)]

    def scratch(x_rows, s1_rows, s2_rows, counts, landing=0):
        refs = [pltpu.VMEM((x_rows, 48, width), BF16)]
        refs += [pltpu.VMEM((2, r, channels, width), F32) for r in (s1_rows, s2_rows)]
        if landing:
            refs += [pltpu.VMEM((3, 3, 3, channels, channels), F32)]
            refs += [pltpu.SemaphoreType.DMA(()), pltpu.SemaphoreType.DMA((landing,))]
        for i, count in enumerate(counts):
            refs += [pltpu.VMEM((1 if i == 2 else 2, count // 2 - 1, 4, 2 * channels, width), BF16)]
        refs += [pltpu.VMEM((2, count, channels, width), F32) for i, count in enumerate(counts) if i != 2]
        return refs

    far = pl.pallas_call(
        far_kernel(rows, half, channels, width),
        out_shape=(*weight_shapes, shape((half - 6, 8, width), F32), *edge_shapes, shape((half + 4, channels, width), F32)),
        in_specs=[SMEM, VMEM, HBM, HBM, VMEM],
        out_specs=(VMEM,) * 13,
        scratch_shapes=scratch(half + 6, half, half, (half + 4, half + 2, half + 2, half, half - 2, half - 4), half + 4),
        compiler_params=params,
        name="far_rows",
    )(info, x_own, target_hbm, w_hbm, w_first.transpose(1, 2, 3, 0))

    y = pl.pallas_call(
        near_kernel(rows, half, channels, width),
        out_shape=shape((half, 8, width), F32),
        in_specs=[SMEM] + [VMEM] * 15,
        out_specs=VMEM,
        scratch_shapes=scratch(8, 6, 6, (8,) * 6),
        compiler_params=params,
        name="near_rows",
    )(info, x_own, halo, *far)
    y = y.transpose(1, 0, 2)[:colours]

    def partner(k):
        return lax.ppermute(y, "step", [(i, i ^ k) for i in range(step_n)])

    difference = image - baseline
    if step_n == 4:
        mine, theirs = y + partner(2), partner(1) + partner(3)
        whole = jnp.where(side == 0, jnp.concatenate([mine, theirs], 1), jnp.concatenate([theirs, mine], 1))
    else:
        order = lax.broadcasted_iota(jnp.int32, (2, 1, 1, 1), 0)
        halves = lax.psum(jnp.where(order == side, y[None], 0.0), "step")
        whole = jnp.concatenate([halves[0], halves[1]], 1)
    return difference * whole / step_n


def solution(mesh):
    in_specs = (P(None, "space", None), P(None, "space", None), P(), P(), P(None, "space", None))
    out_specs = P(None, "space", None)
    return jax.shard_map(body, mesh=mesh, in_specs=in_specs, out_specs=out_specs, check_vma=False)
```

```python
import functools

import jax
import jax.numpy as jnp
from jax import lax
from jax.experimental import pallas as pl
from jax.experimental.pallas import tpu as pltpu
from jax.sharding import PartitionSpec as P

F32, BF16 = jnp.float32, jnp.bfloat16
HALO_X, HALO_T = 6, 4
VMEM = pl.BlockSpec(memory_space=pltpu.VMEM)
HBM = pl.BlockSpec(memory_space=pltpu.HBM)


def dot(a, b):
    return jnp.dot(a, b, preferred_element_type=F32)


def split(value):
    high = value.astype(BF16)
    return high, (value - high.astype(F32)).astype(BF16)


def shift_cols(value, by):
    width = value.shape[-1]
    rolled = pltpu.roll(value, by % width, 1)
    cut = 128 if by > 0 else width - 128
    left, right = rolled[:, :cut], rolled[:, cut:]
    col = lax.broadcasted_iota(jnp.int32, (value.shape[0], 128), 1)
    if by > 0:
        left = jnp.where(col == 0, 0.0, left)
    else:
        right = jnp.where(col == 127, 0.0, right)
    return jnp.concatenate([left, right], 1)


def combine(y, rows):
    return y[rows : 2 * rows] + shift_cols(y[:rows], 1) + shift_cols(y[2 * rows : 3 * rows], -1)


def silu_and_slope(pre):
    sig = 1.0 / (1.0 + jnp.exp(-pre))
    act = pre * sig
    return act, sig + act * (1.0 - sig)


def conv_row(weights, high, low, index):
    stack = lambda ref: ref[index : index + 3].reshape(3 * ref.shape[1], ref.shape[2])
    upper, lower = stack(high), stack(low)
    return dot(weights, jnp.concatenate([upper, upper, lower], 0))


class Maps:
    def __init__(self, refs, base):
        self.high, self.low = refs
        self.base = base

    def put(self, step, row, value):
        self.high[step, row - self.base], self.low[step, row - self.base] = split(value)

    def conv(self, weights, step, row):
        return conv_row(weights, self.high.at[step], self.low.at[step], row - 1 - self.base)

    def copy(self, refs, row, count):
        for part, ref in zip((self.high, self.low), refs):
            ref[...] = part[:, row - self.base : row - self.base + count]

    def load(self, refs, row, count):
        for part, ref in zip((self.high, self.low), refs):
            part[:, row - self.base : row - self.base + count] = ref[...]


def run(spans, weights, xs, x_base, maps, slopes, x_row, t_row, keep, emit, channels, width, g3=None, ready=None, blocks=()):
    w1, wf, wb, w1t = weights
    a1, a2, t, d3, d2, d1 = maps
    s1, s1_base, s2, s2_base = slopes
    rows = lambda name: range(spans[name][0], spans[name][1] + 1)
    inside = lambda name, row: spans[name][0] <= row <= spans[name][1]
    for j in rows("x"):
        x = x_row(j)
        taps = jnp.concatenate([shift_cols(x, 1), x, shift_cols(x, -1)], 0)
        high = taps.astype(BF16).astype(F32)
        xs[j - x_base] = jnp.concatenate([high, taps - high], 0).astype(BF16)
    def first(j):
        stack = xs[j - 1 - x_base : j + 2 - x_base].reshape(3 * xs.shape[1], width)
        pre = dot(w1[...], jnp.concatenate([stack, stack], 0))
        for s in range(2):
            act, slope = silu_and_slope(pre[s * channels : (s + 1) * channels])
            a1.put(s, j, keep(act, j))
            if inside("s1", j):
                s1[s, j - s1_base] = keep(slope, j)

    def second(j):
        for s in range(2):
            if blocks:
                blocks.pop(0)()
            act, slope = silu_and_slope(combine(a1.conv(wf[0], s, j), channels))
            a2.put(s, j, keep(act, j))
            if inside("s2", j):
                s2[s, j - s2_base] = keep(slope, j)

    def target_grad(j):
        return combine(t.conv(wb[2], 0, j), channels)

    def arrive():
        for j in rows("t"):
            t.put(0, j, t_row(j))

    firsts, seconds, thirds = list(rows("a1")), list(rows("a2")), list(rows("d3"))
    early = []
    if not ready:
        arrive()
    for i, j in enumerate(firsts):
        first(j)
        if ready and i == 2:
            ready[0]()
        if ready and i == 7:
            ready[1]()
            arrive()
        if not ready and thirds[i:]:
            g3[thirds[i] - thirds[0]] = target_grad(thirds[i])
            early.append(thirds[i])
        if i >= 3:
            second(seconds.pop(0))
    for j in seconds:
        second(j)
    while blocks:
        blocks.pop(0)()
    for j in thirds:
        grad = g3[j - thirds[0]] if j in early else target_grad(j)
        for s in range(2):
            _, slope = silu_and_slope(combine(a2.conv(wf[1], s, j), channels))
            d3.put(s, j, keep(grad * slope, j))
    for j in rows("d2"):
        for s in range(2):
            d2.put(s, j, combine(d3.conv(wb[1], s, j), channels) * s2[s, j - s2_base])
    for j in rows("d1"):
        for s in range(2):
            d1.put(s, j, combine(d2.conv(wb[0], s, j), channels) * s1[s, j - s1_base])
    for j in rows("out"):
        emit(j, combine(d1.conv(w1t[...], 0, j) + d1.conv(w1t[...], 1, j), 8))


def halves(value):
    high = value.astype(BF16).astype(F32)
    return high, value - high


def wide(value):
    high, low = halves(value)
    return jnp.concatenate([high, low, high], 1).astype(BF16)


def forward_block(tap, w, wf, layer, dx):
    channels = w.shape[-1]
    taps = jnp.concatenate([w[layer, tap(dy), dx] for dy in range(3)], 1)
    wf[layer, pl.ds(dx * channels, channels), :] = wide(taps)


def backward_block(tap, w, wb, layer, dx):
    channels = w.shape[-1]
    taps = jnp.concatenate([w[layer, tap(2 - dy), 2 - dx] for dy in range(3)], 0)
    wb[layer, pl.ds(dx * channels, channels), :] = wide(taps.T)


def prepare_first(tap, w_first, w1, w1t, channels, colours):
    zeros = lambda count: jnp.zeros((count, channels), F32)
    for s in range(2):
        fronts, backs = [], []
        for dy in range(3):
            slots = [
                jnp.concatenate([zeros(4)] * s + [w_first[:, tap(dy), dx, :], zeros(4 - colours)] + [zeros(4)] * (1 - s), 0)
                for dx in range(3)
            ]
            high, low = halves(jnp.concatenate(slots, 0))
            fronts += [high, high]
            backs += [low, jnp.zeros_like(low)]
        w1[pl.ds(s * channels, channels), :] = jnp.concatenate(fronts + backs, 0).T.astype(BF16)
    last = [
        jnp.concatenate(
            sum([[w_first[:, tap(2 - dy), 2 - dx, :], zeros(8 - colours)] for dx in range(3)], []), 0
        )
        for dy in range(3)
    ]
    w1t[...] = wide(jnp.concatenate(last, 1))


def place_on_mesh():
    step = lax.axis_index("step")
    return lax.axis_index("space"), lax.rem(step, 2), lax.div(step, 2)


def pack_kernel(rows, step_n):
    def kernel(image, baseline, target, x_own, send, image_copy, base_copy, sems, row_sems):
        _, side, group = place_on_mesh()
        fractions = [((2 * group + s).astype(F32) + 0.5) * (1.0 / step_n) for s in range(2)]
        channels = target.shape[0]
        copies = []
        for source, landing, i in ((image, image_copy, 0), (baseline, base_copy, 1)):
            copies.append(pltpu.make_async_copy(source, landing, sems.at[i]))
            copies[-1].start()
        for j in range(HALO_T):
            row = jnp.where(side == 0, rows - HALO_T + j, HALO_T - 1 - j)
            place = send.at[pl.ds(channels * j, channels), :]
            copies.append(pltpu.make_async_copy(target.at[:, row, :], place, row_sems.at[j]))
            copies[-1].start()
        copies[0].wait()
        copies[1].wait()
        base, difference = base_copy[...], image_copy[...] - base_copy[...]
        colours = base.shape[0]
        zero = jnp.zeros((4 - colours,) + base.shape[1:], F32)
        for s in range(2):
            x_own[pl.ds(4 * s, colours)] = base + fractions[s] * difference
            x_own[pl.ds(4 * s + colours, 4 - colours)] = zero
        for j in range(HALO_X):
            row = jnp.where(side == 0, rows - HALO_X + j, HALO_X - 1 - j)
            send[pl.ds(HALO_T * channels + 8 * j, 8), :] = x_own[:, row, :]
        for copy in copies[2:]:
            copy.wait()

    return kernel


def spans_of(half):
    near = {"x": (-6, 1), "t": (-4, 3), "a1": (-5, 0), "s1": (-1, 0), "a2": (-4, 1), "s2": (-2, 1)}
    near |= {"d3": (-3, 2), "d2": (-2, 3), "d1": (-1, 4), "out": (0, 5)}
    far = {"x": (0, half + 5), "t": (2, half + 3), "a1": (1, half + 4), "s1": (1, half), "a2": (2, half + 3)}
    far |= {"s2": (2, half + 1), "d3": (3, half + 2), "d2": (4, half + 1), "d1": (5, half), "out": (6, half - 1)}
    return near, far


def fetch_rows(target, landing, sems, row_of):
    copies = []
    for local in range(landing.shape[0]):
        copies.append(pltpu.make_async_copy(target.at[:, row_of(local), :], landing.at[local], sems.at[local]))
        copies[-1].start()
    return lambda local: copies[local].wait()


def far_kernel(rows, half, channels, width):
    def kernel(x_own, target, w, w_first, *refs):
        w1, wf, wb, w1t, out = refs[:5]
        edges, (e1, e2) = refs[5:15], refs[15:17]
        t_rows = refs[17]
        xs, s1, s2, t_sems = refs[18:22]
        work = refs[22:]
        _, side, _ = place_on_mesh()
        row_of = lambda local: jnp.where(side == 0, local, rows - 1 - local)
        t_row = fetch_rows(target, t_rows, t_sems, row_of)
        tap = lambda dy: jnp.where(side == 1, 2 - dy, dy)
        prepare_first(tap, w_first, w1, w1t, channels, w_first.shape[0])
        backward = lambda layer: [functools.partial(backward_block, tap, w, wb, layer, dx) for dx in range(3)]
        blocks = backward(0)

        def ready():
            for dx in range(3):
                forward_block(tap, w, wf, 0, dx)

        def landed():
            for local in range(t_rows.shape[0]):
                t_row(local)
            blocks.extend(functools.partial(forward_block, tap, w, wf, 1, dx) for dx in range(3))
            blocks.extend(backward(2) + backward(1))

        spans = spans_of(half)[1]
        maps = [Maps(work[2 * i : 2 * i + 2], b) for i, b in enumerate((1, 2, 2, 3, 4, 5))]

        def emit(j, value):
            out[j - spans["out"][0]] = value

        run(
            spans, (w1, wf, wb, w1t), xs, 0, maps, (s1, 1, s2, 2),
            lambda j: x_own[:, row_of(j), :], lambda j: t_rows[j],
            lambda value, j: value, emit, channels, width, None, (ready, landed), blocks,
        )
        a1, a2, _, d3, d2, d1 = maps
        for i, (m, row) in enumerate(((a1, 1), (a2, 2), (d3, 3), (d2, 4), (d1, 5))):
            m.copy(edges[2 * i : 2 * i + 2], row, 2)
        e1[...] = s1[:, 0:4]
        e2[...] = s2[:, 0:2]

    return kernel


def near_kernel(rows, half, channels, width, space_n):
    def kernel(x_own, halo, *refs):
        w1, wf, wb, w1t, far_out = refs[:5]
        edges, (e1, e2) = refs[5:15], refs[15:17]
        t_rows, out = refs[17:19]
        xs, s1, s2 = refs[19:22]
        g3, work = refs[22], refs[23:]
        space, side, _ = place_on_mesh()
        exists = jnp.where(side == 0, space, space_n - 1 - space) > 0
        row_of = lambda local: jnp.where(side == 0, local, rows - 1 - local)
        place = lambda local: jnp.where(side == 0, local, half - 1 - local)
        spans = spans_of(half)[0]
        maps = [Maps(work[2 * i : 2 * i + 2], b) for i, b in enumerate((-5, -4, -4, -3, -2, -1))]
        a1, a2, _, d3, d2, d1 = maps
        for i, (m, row) in enumerate(((a1, 1), (a2, 2), (d3, 3), (d2, 4), (d1, 5))):
            m.load(edges[2 * i : 2 * i + 2], row, 2)
        s1[:, 2:6] = e1[...]
        s2[:, 4:6] = e2[...]
        for j in range(6, half):
            out[place(j)] = far_out[j - 6]

        def x_row(j):
            if j < 0:
                return halo[pl.ds(HALO_T * channels + 8 * (j + HALO_X), 8), :]
            return x_own[:, row_of(j), :]

        def t_row(j):
            if j < 0:
                return halo[pl.ds(channels * (j + HALO_T), channels), :]
            return t_rows[j]

        def keep(value, j):
            return jnp.where(exists, value, 0.0) if j < 0 else value

        def emit(j, value):
            out[place(j)] = value

        run(
            spans, (w1, wf, wb, w1t), xs, -6, maps, (s1, -1, s2, -2),
            x_row, t_row, keep, emit, channels, width, g3,
        )

    return kernel


def body(image, baseline, w_first, w_rest, target):
    colours, rows, width = image.shape
    channels = target.shape[0]
    half = rows // 2
    space_n, step_n = lax.axis_size("space"), lax.axis_size("step")
    step = lax.axis_index("step")
    side = step % 2
    in_hbm = lambda array: pltpu.with_memory_space_constraint(array, pltpu.HBM)
    target_hbm = in_hbm(target)
    w_taps = w_rest.transpose(0, 3, 4, 1, 2)
    params = pltpu.CompilerParams(vmem_limit_bytes=40 << 20)
    shape = jax.ShapeDtypeStruct

    x_own, send = pl.pallas_call(
        pack_kernel(rows, step_n),
        out_shape=(shape((8, rows, width), F32), shape((HALO_T * channels + HALO_X * 8, width), F32)),
        in_specs=[HBM, HBM, HBM],
        out_specs=(VMEM, VMEM),
        scratch_shapes=[pltpu.VMEM((colours, rows, width), F32)] * 2
        + [pltpu.SemaphoreType.DMA((2,)), pltpu.SemaphoreType.DMA((HALO_T,))],
        compiler_params=params,
        name="pack_edges",
    )(in_hbm(image), in_hbm(baseline), target_hbm)

    pairs = []
    for i in range(space_n):
        for s in range(step_n):
            source = i + 1 if s % 2 else i - 1
            if 0 <= source < space_n:
                pairs.append((source * step_n + s, i * step_n + s))
    halo = lax.ppermute(send, ("space", "step"), pairs)

    n = 3 * channels
    weight_shapes = [
        shape((2 * channels, 288), BF16),
        shape((2, n, 3 * n), BF16),
        shape((3, n, 3 * n), BF16),
        shape((24, 3 * n), BF16),
    ]
    edge_shapes = [shape((2, 2, channels, width), BF16)] * 10
    edge_shapes += [shape((2, 4, channels, width), F32), shape((2, 2, channels, width), F32)]

    def scratch(x_rows, s1_rows, s2_rows, counts, landing=0):
        refs = [pltpu.VMEM((x_rows, 48, width), BF16)]
        refs += [pltpu.VMEM((2, r, channels, width), F32) for r in (s1_rows, s2_rows)]
        if landing:
            refs += [pltpu.SemaphoreType.DMA((landing,))]
        else:
            refs += [pltpu.VMEM((6, channels, width), F32)]
        for i, count in enumerate(counts):
            refs += [pltpu.VMEM((1 if i == 2 else 2, count, channels, width), BF16)] * 2
        return refs

    far = pl.pallas_call(
        far_kernel(rows, half, channels, width),
        out_shape=(*weight_shapes, shape((half - 6, 8, width), F32), *edge_shapes, shape((half + 4, channels, width), F32)),
        in_specs=[VMEM, HBM, VMEM, VMEM],
        out_specs=(VMEM,) * 18,
        scratch_shapes=scratch(half + 6, half, half, (half + 4, half + 2, half + 2, half, half - 2, half - 4), half + 4),
        compiler_params=params,
        name="far_rows",
    )(x_own, target_hbm, w_taps, w_first.transpose(1, 2, 3, 0))

    y = pl.pallas_call(
        near_kernel(rows, half, channels, width, space_n),
        out_shape=shape((half, 8, width), F32),
        in_specs=[VMEM] * 20,
        out_specs=VMEM,
        scratch_shapes=scratch(8, 6, 6, (8,) * 6),
        compiler_params=params,
        name="near_rows",
    )(x_own, halo, *far)
    y = y.transpose(1, 0, 2)[:colours]

    def partner(k):
        return lax.ppermute(y, "step", [(i, i ^ k) for i in range(step_n)])

    difference = image - baseline
    if step_n == 4:
        mine, theirs = y + partner(2), partner(1) + partner(3)
        whole = jnp.where(side == 0, jnp.concatenate([mine, theirs], 1), jnp.concatenate([theirs, mine], 1))
    else:
        order = lax.broadcasted_iota(jnp.int32, (2, 1, 1, 1), 0)
        halves = lax.psum(jnp.where(order == side, y[None], 0.0), "step")
        whole = jnp.concatenate([halves[0], halves[1]], 1)
    return difference * whole / step_n


def solution(mesh):
    in_specs = (P(None, "space", None), P(None, "space", None), P(), P(), P(None, "space", None))
    out_specs = P(None, "space", None)
    return jax.shard_map(body, mesh=mesh, in_specs=in_specs, out_specs=out_specs, check_vma=False)
```

```python
import functools

import jax
import jax.numpy as jnp
from jax import lax
from jax.experimental import pallas as pl
from jax.experimental.pallas import tpu as pltpu
from jax.sharding import PartitionSpec as P

F32, BF16 = jnp.float32, jnp.bfloat16
HALO_X, HALO_T = 6, 4
VMEM = pl.BlockSpec(memory_space=pltpu.VMEM)
HBM = pl.BlockSpec(memory_space=pltpu.HBM)


def dot(a, b):
    return jnp.dot(a, b, preferred_element_type=F32)


def split(value):
    high = value.astype(BF16)
    return high, (value - high.astype(F32)).astype(BF16)


def shift_cols(value, by):
    width = value.shape[-1]
    rolled = pltpu.roll(value, by % width, 1)
    cut = 128 if by > 0 else width - 128
    left, right = rolled[:, :cut], rolled[:, cut:]
    col = lax.broadcasted_iota(jnp.int32, (value.shape[0], 128), 1)
    if by > 0:
        left = jnp.where(col == 0, 0.0, left)
    else:
        right = jnp.where(col == 127, 0.0, right)
    return jnp.concatenate([left, right], 1)


def combine(y, rows):
    return y[rows : 2 * rows] + shift_cols(y[:rows], 1) + shift_cols(y[2 * rows : 3 * rows], -1)


def silu_and_slope(pre):
    sig = 1.0 / (1.0 + jnp.exp(-pre))
    act = pre * sig
    return act, sig + act * (1.0 - sig)


def conv_row(weights, high, low, index):
    stack = lambda ref: ref[index : index + 3].reshape(3 * ref.shape[1], ref.shape[2])
    upper, lower = stack(high), stack(low)
    return dot(weights, jnp.concatenate([upper, upper, lower], 0))


class Maps:
    def __init__(self, refs, base):
        self.high, self.low = refs
        self.base = base

    def put(self, step, row, value):
        self.high[step, row - self.base], self.low[step, row - self.base] = split(value)

    def conv(self, weights, step, row):
        return conv_row(weights, self.high.at[step], self.low.at[step], row - 1 - self.base)

    def copy(self, refs, row, count):
        for part, ref in zip((self.high, self.low), refs):
            ref[...] = part[:, row - self.base : row - self.base + count]

    def load(self, refs, row, count):
        for part, ref in zip((self.high, self.low), refs):
            part[:, row - self.base : row - self.base + count] = ref[...]


def run(spans, weights, xs, x_base, maps, slopes, x_row, t_row, keep, emit, channels, width, g3=None, ready=None, blocks=()):
    w1, wf, wb, w1t = weights
    a1, a2, t, d3, d2, d1 = maps
    s1, s1_base, s2, s2_base = slopes
    rows = lambda name: range(spans[name][0], spans[name][1] + 1)
    inside = lambda name, row: spans[name][0] <= row <= spans[name][1]
    for j in rows("x"):
        x = x_row(j)
        taps = jnp.concatenate([shift_cols(x, 1), x, shift_cols(x, -1)], 0)
        high = taps.astype(BF16).astype(F32)
        xs[j - x_base] = jnp.concatenate([high, taps - high], 0).astype(BF16)
    def first(j):
        stack = xs[j - 1 - x_base : j + 2 - x_base].reshape(3 * xs.shape[1], width)
        pre = dot(w1[...], jnp.concatenate([stack, stack], 0))
        for s in range(2):
            act, slope = silu_and_slope(pre[s * channels : (s + 1) * channels])
            a1.put(s, j, keep(act, j))
            if inside("s1", j):
                s1[s, j - s1_base] = keep(slope, j)

    def second(j):
        for s in range(2):
            if blocks:
                blocks.pop(0)()
            act, slope = silu_and_slope(combine(a1.conv(wf[0], s, j), channels))
            a2.put(s, j, keep(act, j))
            if inside("s2", j):
                s2[s, j - s2_base] = keep(slope, j)

    def target_grad(j):
        return combine(t.conv(wb[2], 0, j), channels)

    def arrive():
        for j in rows("t"):
            t.put(0, j, t_row(j))

    firsts, seconds, thirds = list(rows("a1")), list(rows("a2")), list(rows("d3"))
    early = []
    if not ready:
        arrive()
    for i, j in enumerate(firsts):
        first(j)
        if ready and i == 2:
            ready[0]()
        if ready and i == 7:
            ready[1]()
            arrive()
        if not ready and thirds[i:]:
            g3[thirds[i] - thirds[0]] = target_grad(thirds[i])
            early.append(thirds[i])
        if i >= 3:
            second(seconds.pop(0))
    for j in seconds:
        second(j)
    while blocks:
        blocks.pop(0)()
    for j in thirds:
        grad = g3[j - thirds[0]] if j in early else target_grad(j)
        for s in range(2):
            _, slope = silu_and_slope(combine(a2.conv(wf[1], s, j), channels))
            d3.put(s, j, keep(grad * slope, j))
    for j in rows("d2"):
        for s in range(2):
            d2.put(s, j, combine(d3.conv(wb[1], s, j), channels) * s2[s, j - s2_base])
    for j in rows("d1"):
        grads = [combine(d2.conv(wb[0], s, j), channels) * s1[s, j - s1_base] for s in range(2)]
        d1.put(0, j, grads[0] + grads[1])
    for j in rows("out"):
        emit(j, combine(d1.conv(w1t[...], 0, j), 8))


def halves(value):
    high = value.astype(BF16).astype(F32)
    return high, value - high


def wide(value):
    high, low = halves(value)
    return jnp.concatenate([high, low, high], 1).astype(BF16)


def forward_block(tap, w, wf, layer, dx):
    channels = w.shape[-1]
    taps = jnp.concatenate([w[layer, tap(dy), dx] for dy in range(3)], 1)
    wf[layer, pl.ds(dx * channels, channels), :] = wide(taps)


def backward_block(tap, w, wb, layer, dx):
    channels = w.shape[-1]
    taps = jnp.concatenate([w[layer, tap(2 - dy), 2 - dx] for dy in range(3)], 0)
    wb[layer, pl.ds(dx * channels, channels), :] = wide(taps.T)


def prepare_first(tap, w_first, w1, w1t, channels, colours):
    zeros = lambda count: jnp.zeros((count, channels), F32)
    for s in range(2):
        fronts, backs = [], []
        for dy in range(3):
            slots = [
                jnp.concatenate([zeros(4)] * s + [w_first[:, tap(dy), dx, :], zeros(4 - colours)] + [zeros(4)] * (1 - s), 0)
                for dx in range(3)
            ]
            high, low = halves(jnp.concatenate(slots, 0))
            fronts += [high, high]
            backs += [low, jnp.zeros_like(low)]
        w1[pl.ds(s * channels, channels), :] = jnp.concatenate(fronts + backs, 0).T.astype(BF16)
    last = [
        jnp.concatenate(
            sum([[w_first[:, tap(2 - dy), 2 - dx, :], zeros(8 - colours)] for dx in range(3)], []), 0
        )
        for dy in range(3)
    ]
    w1t[...] = wide(jnp.concatenate(last, 1))


def place_on_mesh():
    step = lax.axis_index("step")
    return lax.axis_index("space"), lax.rem(step, 2), lax.div(step, 2)


def pack_kernel(rows, step_n):
    def kernel(image, baseline, target, x_own, send, image_copy, base_copy, sems, row_sems):
        _, side, group = place_on_mesh()
        fractions = [((2 * group + s).astype(F32) + 0.5) * (1.0 / step_n) for s in range(2)]
        channels = target.shape[0]
        copies = []
        for source, landing, i in ((image, image_copy, 0), (baseline, base_copy, 1)):
            copies.append(pltpu.make_async_copy(source, landing, sems.at[i]))
            copies[-1].start()
        for j in range(HALO_T):
            row = jnp.where(side == 0, rows - HALO_T + j, HALO_T - 1 - j)
            place = send.at[pl.ds(channels * j, channels), :]
            copies.append(pltpu.make_async_copy(target.at[:, row, :], place, row_sems.at[j]))
            copies[-1].start()
        copies[0].wait()
        copies[1].wait()
        base, difference = base_copy[...], image_copy[...] - base_copy[...]
        colours = base.shape[0]
        zero = jnp.zeros((4 - colours,) + base.shape[1:], F32)
        for s in range(2):
            x_own[pl.ds(4 * s, colours)] = base + fractions[s] * difference
            x_own[pl.ds(4 * s + colours, 4 - colours)] = zero
        for j in range(HALO_X):
            row = jnp.where(side == 0, rows - HALO_X + j, HALO_X - 1 - j)
            send[pl.ds(HALO_T * channels + 8 * j, 8), :] = x_own[:, row, :]
        for copy in copies[2:]:
            copy.wait()

    return kernel


def spans_of(half):
    near = {"x": (-6, 1), "t": (-4, 3), "a1": (-5, 0), "s1": (-1, 0), "a2": (-4, 1), "s2": (-2, 1)}
    near |= {"d3": (-3, 2), "d2": (-2, 3), "d1": (-1, 4), "out": (0, 5)}
    far = {"x": (0, half + 5), "t": (2, half + 3), "a1": (1, half + 4), "s1": (1, half), "a2": (2, half + 3)}
    far |= {"s2": (2, half + 1), "d3": (3, half + 2), "d2": (4, half + 1), "d1": (5, half), "out": (6, half - 1)}
    return near, far


def fetch_rows(target, landing, sems, row_of):
    copies = []
    for local in range(landing.shape[0]):
        copies.append(pltpu.make_async_copy(target.at[:, row_of(local), :], landing.at[local], sems.at[local]))
        copies[-1].start()
    return lambda local: copies[local].wait()


def far_kernel(rows, half, channels, width):
    def kernel(x_own, target, w, w_first, *refs):
        w1, wf, wb, w1t, out = refs[:5]
        edges, (e1, e2) = refs[5:15], refs[15:17]
        t_rows = refs[17]
        xs, s1, s2, t_sems = refs[18:22]
        work = refs[22:]
        _, side, _ = place_on_mesh()
        row_of = lambda local: jnp.where(side == 0, local, rows - 1 - local)
        t_row = fetch_rows(target, t_rows, t_sems, row_of)
        tap = lambda dy: jnp.where(side == 1, 2 - dy, dy)
        prepare_first(tap, w_first, w1, w1t, channels, w_first.shape[0])
        backward = lambda layer: [functools.partial(backward_block, tap, w, wb, layer, dx) for dx in range(3)]
        blocks = backward(0)

        def ready():
            for dx in range(3):
                forward_block(tap, w, wf, 0, dx)

        def landed():
            for local in range(t_rows.shape[0]):
                t_row(local)
            blocks.extend(functools.partial(forward_block, tap, w, wf, 1, dx) for dx in range(3))
            blocks.extend(backward(2) + backward(1))

        spans = spans_of(half)[1]
        maps = [Maps(work[2 * i : 2 * i + 2], b) for i, b in enumerate((1, 2, 2, 3, 4, 5))]

        def emit(j, value):
            out[j - spans["out"][0]] = value

        run(
            spans, (w1, wf, wb, w1t), xs, 0, maps, (s1, 1, s2, 2),
            lambda j: x_own[:, row_of(j), :], lambda j: t_rows[j],
            lambda value, j: value, emit, channels, width, None, (ready, landed), blocks,
        )
        a1, a2, _, d3, d2, d1 = maps
        for i, (m, row) in enumerate(((a1, 1), (a2, 2), (d3, 3), (d2, 4), (d1, 5))):
            m.copy(edges[2 * i : 2 * i + 2], row, 2)
        e1[...] = s1[:, 0:4]
        e2[...] = s2[:, 0:2]

    return kernel


def near_kernel(rows, half, channels, width, space_n):
    def kernel(x_own, halo, *refs):
        w1, wf, wb, w1t, far_out = refs[:5]
        edges, (e1, e2) = refs[5:15], refs[15:17]
        t_rows, out = refs[17:19]
        xs, s1, s2 = refs[19:22]
        g3, work = refs[22], refs[23:]
        space, side, _ = place_on_mesh()
        exists = jnp.where(side == 0, space, space_n - 1 - space) > 0
        row_of = lambda local: jnp.where(side == 0, local, rows - 1 - local)
        place = lambda local: jnp.where(side == 0, local, half - 1 - local)
        spans = spans_of(half)[0]
        maps = [Maps(work[2 * i : 2 * i + 2], b) for i, b in enumerate((-5, -4, -4, -3, -2, -1))]
        a1, a2, _, d3, d2, d1 = maps
        for i, (m, row) in enumerate(((a1, 1), (a2, 2), (d3, 3), (d2, 4), (d1, 5))):
            m.load(edges[2 * i : 2 * i + 2], row, 2)
        s1[:, 2:6] = e1[...]
        s2[:, 4:6] = e2[...]
        for j in range(6, half):
            out[place(j)] = far_out[j - 6]

        def x_row(j):
            if j < 0:
                return halo[pl.ds(HALO_T * channels + 8 * (j + HALO_X), 8), :]
            return x_own[:, row_of(j), :]

        def t_row(j):
            if j < 0:
                return halo[pl.ds(channels * (j + HALO_T), channels), :]
            return t_rows[j]

        def keep(value, j):
            return jnp.where(exists, value, 0.0) if j < 0 else value

        def emit(j, value):
            out[place(j)] = value

        run(
            spans, (w1, wf, wb, w1t), xs, -6, maps, (s1, -1, s2, -2),
            x_row, t_row, keep, emit, channels, width, g3,
        )

    return kernel


def body(image, baseline, w_first, w_rest, target):
    colours, rows, width = image.shape
    channels = target.shape[0]
    half = rows // 2
    space_n, step_n = lax.axis_size("space"), lax.axis_size("step")
    step = lax.axis_index("step")
    side = step % 2
    in_hbm = lambda array: pltpu.with_memory_space_constraint(array, pltpu.HBM)
    target_hbm = in_hbm(target)
    w_taps = w_rest.transpose(0, 3, 4, 1, 2)
    params = pltpu.CompilerParams(vmem_limit_bytes=40 << 20)
    shape = jax.ShapeDtypeStruct

    x_own, send = pl.pallas_call(
        pack_kernel(rows, step_n),
        out_shape=(shape((8, rows, width), F32), shape((HALO_T * channels + HALO_X * 8, width), F32)),
        in_specs=[HBM, HBM, HBM],
        out_specs=(VMEM, VMEM),
        scratch_shapes=[pltpu.VMEM((colours, rows, width), F32)] * 2
        + [pltpu.SemaphoreType.DMA((2,)), pltpu.SemaphoreType.DMA((HALO_T,))],
        compiler_params=params,
        name="pack_edges",
    )(in_hbm(image), in_hbm(baseline), target_hbm)

    pairs = []
    for i in range(space_n):
        for s in range(step_n):
            source = i + 1 if s % 2 else i - 1
            if 0 <= source < space_n:
                pairs.append((source * step_n + s, i * step_n + s))
    halo = lax.ppermute(send, ("space", "step"), pairs)

    n = 3 * channels
    weight_shapes = [
        shape((2 * channels, 288), BF16),
        shape((2, n, 3 * n), BF16),
        shape((3, n, 3 * n), BF16),
        shape((24, 3 * n), BF16),
    ]
    edge_shapes = [shape((2, 2, channels, width), BF16)] * 8 + [shape((1, 2, channels, width), BF16)] * 2
    edge_shapes += [shape((2, 4, channels, width), F32), shape((2, 2, channels, width), F32)]

    def scratch(x_rows, s1_rows, s2_rows, counts, landing=0):
        refs = [pltpu.VMEM((x_rows, 48, width), BF16)]
        refs += [pltpu.VMEM((2, r, channels, width), F32) for r in (s1_rows, s2_rows)]
        if landing:
            refs += [pltpu.SemaphoreType.DMA((landing,))]
        else:
            refs += [pltpu.VMEM((6, channels, width), F32)]
        for i, count in enumerate(counts):
            refs += [pltpu.VMEM((1 if i in (2, 5) else 2, count, channels, width), BF16)] * 2
        return refs

    far = pl.pallas_call(
        far_kernel(rows, half, channels, width),
        out_shape=(*weight_shapes, shape((half - 6, 8, width), F32), *edge_shapes, shape((half + 4, channels, width), F32)),
        in_specs=[VMEM, HBM, VMEM, VMEM],
        out_specs=(VMEM,) * 18,
        scratch_shapes=scratch(half + 6, half, half, (half + 4, half + 2, half + 2, half, half - 2, half - 4), half + 4),
        compiler_params=params,
        name="far_rows",
    )(x_own, target_hbm, w_taps, w_first.transpose(1, 2, 3, 0))

    y = pl.pallas_call(
        near_kernel(rows, half, channels, width, space_n),
        out_shape=shape((half, 8, width), F32),
        in_specs=[VMEM] * 20,
        out_specs=VMEM,
        scratch_shapes=scratch(8, 6, 6, (8,) * 6),
        compiler_params=params,
        name="near_rows",
    )(x_own, halo, *far)
    y = y.transpose(1, 0, 2)[:colours]

    def partner(value, k):
        return lax.ppermute(value, "step", [(i, i ^ k) for i in range(step_n)])

    difference = image - baseline
    if step_n == 4:
        mine = y + partner(y, 2)
        theirs = partner(mine, 1)
        whole = jnp.where(side == 0, jnp.concatenate([mine, theirs], 1), jnp.concatenate([theirs, mine], 1))
    else:
        order = lax.broadcasted_iota(jnp.int32, (2, 1, 1, 1), 0)
        halves = lax.psum(jnp.where(order == side, y[None], 0.0), "step")
        whole = jnp.concatenate([halves[0], halves[1]], 1)
    return difference * whole / step_n


def solution(mesh):
    in_specs = (P(None, "space", None), P(None, "space", None), P(), P(), P(None, "space", None))
    out_specs = P(None, "space", None)
    return jax.shard_map(body, mesh=mesh, in_specs=in_specs, out_specs=out_specs, check_vma=False)
```

```python
import functools

import jax
import jax.numpy as jnp
from jax import lax
from jax.experimental import pallas as pl
from jax.experimental.pallas import tpu as pltpu
from jax.sharding import PartitionSpec as P

F32, BF16 = jnp.float32, jnp.bfloat16
HALO_X, HALO_T = 6, 4
VMEM = pl.BlockSpec(memory_space=pltpu.VMEM)
HBM = pl.BlockSpec(memory_space=pltpu.HBM)


def dot(a, b):
    return jnp.dot(a, b, preferred_element_type=F32)


def split(value):
    high = value.astype(BF16)
    return high, (value - high.astype(F32)).astype(BF16)


def shift_cols(value, by):
    width = value.shape[-1]
    rolled = pltpu.roll(value, by % width, 1)
    cut = 128 if by > 0 else width - 128
    left, right = rolled[:, :cut], rolled[:, cut:]
    col = lax.broadcasted_iota(jnp.int32, (value.shape[0], 128), 1)
    if by > 0:
        left = jnp.where(col == 0, 0.0, left)
    else:
        right = jnp.where(col == 127, 0.0, right)
    return jnp.concatenate([left, right], 1)


def combine(y, rows):
    return y[rows : 2 * rows] + shift_cols(y[:rows], 1) + shift_cols(y[2 * rows : 3 * rows], -1)


def silu_and_slope(pre):
    sig = 1.0 / (1.0 + jnp.exp(-pre))
    act = pre * sig
    return act, sig + act * (1.0 - sig)


def conv_row(weights, high, low, index):
    stack = lambda ref: ref[index : index + 3].reshape(3 * ref.shape[1], ref.shape[2])
    upper, lower = stack(high), stack(low)
    return dot(weights, jnp.concatenate([upper, upper, lower], 0))


class Maps:
    def __init__(self, refs, base):
        self.high, self.low = refs
        self.base = base

    def put(self, step, row, value):
        self.high[step, row - self.base], self.low[step, row - self.base] = split(value)

    def conv(self, weights, step, row):
        return conv_row(weights, self.high.at[step], self.low.at[step], row - 1 - self.base)

    def copy(self, refs, row, count):
        for part, ref in zip((self.high, self.low), refs):
            ref[...] = part[:, row - self.base : row - self.base + count]

    def load(self, refs, row, count):
        for part, ref in zip((self.high, self.low), refs):
            part[:, row - self.base : row - self.base + count] = ref[...]


def run(spans, weights, xs, x_base, maps, slopes, x_row, t_row, keep, emit, channels, width, g3=None, ready=None, blocks=()):
    w1, wf, wb, w1t = weights
    a1, a2, t, d3, d2, d1 = maps
    s1, s1_base, s2, s2_base = slopes
    rows = lambda name: range(spans[name][0], spans[name][1] + 1)
    inside = lambda name, row: spans[name][0] <= row <= spans[name][1]
    for j in rows("x"):
        x = x_row(j)
        taps = jnp.concatenate([shift_cols(x, 1), x, shift_cols(x, -1)], 0)
        high = taps.astype(BF16).astype(F32)
        xs[j - x_base] = jnp.concatenate([high, taps - high], 0).astype(BF16)
    def first(j):
        stack = xs[j - 1 - x_base : j + 2 - x_base].reshape(3 * xs.shape[1], width)
        pre = dot(w1[...], jnp.concatenate([stack, stack], 0))
        for s in range(2):
            act, slope = silu_and_slope(pre[s * channels : (s + 1) * channels])
            a1.put(s, j, keep(act, j))
            if inside("s1", j):
                s1[s, j - s1_base] = keep(slope, j)

    def second(j):
        for s in range(2):
            if blocks:
                blocks.pop(0)()
            act, slope = silu_and_slope(combine(a1.conv(wf[0], s, j), channels))
            a2.put(s, j, keep(act, j))
            if inside("s2", j):
                s2[s, j - s2_base] = keep(slope, j)

    def target_grad(j):
        return combine(t.conv(wb[2], 0, j), channels)

    def arrive():
        for j in rows("t"):
            t.put(0, j, t_row(j))

    firsts, seconds, thirds = list(rows("a1")), list(rows("a2")), list(rows("d3"))
    early = []
    if not ready:
        arrive()
    for i, j in enumerate(firsts):
        first(j)
        if ready and i == 2:
            ready[0]()
        if ready and i == 7:
            ready[1]()
            arrive()
        if not ready and thirds[i:]:
            g3[thirds[i] - thirds[0]] = target_grad(thirds[i])
            early.append(thirds[i])
        if i >= 3:
            second(seconds.pop(0))
    for j in seconds:
        second(j)
    while blocks:
        blocks.pop(0)()
    for j in thirds:
        grad = g3[j - thirds[0]] if j in early else target_grad(j)
        for s in range(2):
            _, slope = silu_and_slope(combine(a2.conv(wf[1], s, j), channels))
            d3.put(s, j, keep(grad * slope, j))
    for j in rows("d2"):
        for s in range(2):
            d2.put(s, j, combine(d3.conv(wb[1], s, j), channels) * s2[s, j - s2_base])
    for j in rows("d1"):
        grads = [combine(d2.conv(wb[0], s, j), channels) * s1[s, j - s1_base] for s in range(2)]
        d1.put(0, j, grads[0] + grads[1])
    for j in rows("out"):
        emit(j, combine(d1.conv(w1t[...], 0, j), 8))


def halves(value):
    high = value.astype(BF16).astype(F32)
    return high, value - high


def wide(value):
    high, low = halves(value)
    return jnp.concatenate([high, low, high], 1).astype(BF16)


def forward_block(tap, w, wf, layer, dx):
    channels = w.shape[-1]
    taps = jnp.concatenate([w[layer, tap(dy), dx] for dy in range(3)], 1)
    wf[layer, pl.ds(dx * channels, channels), :] = wide(taps)


def backward_block(tap, w, wb, layer, dx):
    channels = w.shape[-1]
    taps = jnp.concatenate([w[layer, tap(2 - dy), 2 - dx] for dy in range(3)], 0)
    wb[layer, pl.ds(dx * channels, channels), :] = wide(taps.T)


def prepare_first(tap, w_first, w1, w1t, channels, colours):
    zeros = lambda count: jnp.zeros((count, channels), F32)
    for s in range(2):
        fronts, backs = [], []
        for dy in range(3):
            slots = [
                jnp.concatenate([zeros(4)] * s + [w_first[:, tap(dy), dx, :], zeros(4 - colours)] + [zeros(4)] * (1 - s), 0)
                for dx in range(3)
            ]
            high, low = halves(jnp.concatenate(slots, 0))
            fronts += [high, high]
            backs += [low, jnp.zeros_like(low)]
        w1[pl.ds(s * channels, channels), :] = jnp.concatenate(fronts + backs, 0).T.astype(BF16)
    last = [
        jnp.concatenate(
            sum([[w_first[:, tap(2 - dy), 2 - dx, :], zeros(8 - colours)] for dx in range(3)], []), 0
        )
        for dy in range(3)
    ]
    w1t[...] = wide(jnp.concatenate(last, 1))


def place_on_mesh():
    step = lax.axis_index("step")
    return lax.axis_index("space"), lax.rem(step, 2), lax.div(step, 2)


def pack_kernel(rows, step_n):
    def kernel(image, baseline, target, x_own, send, image_copy, base_copy, sems, row_sems):
        _, side, group = place_on_mesh()
        fractions = [((2 * group + s).astype(F32) + 0.5) * (1.0 / step_n) for s in range(2)]
        channels = target.shape[0]
        copies = []
        for j in range(HALO_T):
            row = jnp.where(side == 0, rows - HALO_T + j, HALO_T - 1 - j)
            place = send.at[pl.ds(channels * j, channels), :]
            copies.append(pltpu.make_async_copy(target.at[:, row, :], place, row_sems.at[j]))
        for source, landing, i in ((image, image_copy, 0), (baseline, base_copy, 1)):
            copies.append(pltpu.make_async_copy(source, landing, sems.at[i]))
        for copy in copies:
            copy.start()
        copies[-2].wait()
        copies[-1].wait()
        base, difference = base_copy[...], image_copy[...] - base_copy[...]
        colours = base.shape[0]
        zero = jnp.zeros((4 - colours,) + base.shape[1:], F32)
        for s in range(2):
            x_own[pl.ds(4 * s, colours)] = base + fractions[s] * difference
            x_own[pl.ds(4 * s + colours, 4 - colours)] = zero
        for j in range(HALO_X):
            row = jnp.where(side == 0, rows - HALO_X + j, HALO_X - 1 - j)
            send[pl.ds(HALO_T * channels + 8 * j, 8), :] = x_own[:, row, :]
        for copy in copies[:-2]:
            copy.wait()

    return kernel


def spans_of(half):
    near = {"x": (-6, 1), "t": (-4, 3), "a1": (-5, 0), "s1": (-1, 0), "a2": (-4, 1), "s2": (-2, 1)}
    near |= {"d3": (-3, 2), "d2": (-2, 3), "d1": (-1, 4), "out": (0, 5)}
    far = {"x": (0, half + 5), "t": (2, half + 3), "a1": (1, half + 4), "s1": (1, half), "a2": (2, half + 3)}
    far |= {"s2": (2, half + 1), "d3": (3, half + 2), "d2": (4, half + 1), "d1": (5, half), "out": (6, half - 1)}
    return near, far


def fetch_rows(target, landing, sems, row_of):
    copies = []
    for local in range(landing.shape[0]):
        copies.append(pltpu.make_async_copy(target.at[:, row_of(local), :], landing.at[local], sems.at[local]))
        copies[-1].start()
    return lambda local: copies[local].wait()


def far_kernel(rows, half, channels, width):
    def kernel(x_own, target, w, w_first, *refs):
        w1, wf, wb, w1t, out = refs[:5]
        edges, (e1, e2) = refs[5:15], refs[15:17]
        t_rows = refs[17]
        xs, s1, s2, t_sems = refs[18:22]
        work = refs[22:]
        _, side, _ = place_on_mesh()
        row_of = lambda local: jnp.where(side == 0, local, rows - 1 - local)
        t_row = fetch_rows(target, t_rows, t_sems, row_of)
        tap = lambda dy: jnp.where(side == 1, 2 - dy, dy)
        prepare_first(tap, w_first, w1, w1t, channels, w_first.shape[0])
        backward = lambda layer: [functools.partial(backward_block, tap, w, wb, layer, dx) for dx in range(3)]
        blocks = backward(0)

        def ready():
            for dx in range(3):
                forward_block(tap, w, wf, 0, dx)

        def landed():
            for local in range(t_rows.shape[0]):
                t_row(local)
            blocks.extend(functools.partial(forward_block, tap, w, wf, 1, dx) for dx in range(3))
            blocks.extend(backward(2) + backward(1))

        spans = spans_of(half)[1]
        maps = [Maps(work[2 * i : 2 * i + 2], b) for i, b in enumerate((1, 2, 2, 3, 4, 5))]

        def emit(j, value):
            out[j - spans["out"][0]] = value

        run(
            spans, (w1, wf, wb, w1t), xs, 0, maps, (s1, 1, s2, 2),
            lambda j: x_own[:, row_of(j), :], lambda j: t_rows[j],
            lambda value, j: value, emit, channels, width, None, (ready, landed), blocks,
        )
        a1, a2, _, d3, d2, d1 = maps
        for i, (m, row) in enumerate(((a1, 1), (a2, 2), (d3, 3), (d2, 4), (d1, 5))):
            m.copy(edges[2 * i : 2 * i + 2], row, 2)
        e1[...] = s1[:, 0:4]
        e2[...] = s2[:, 0:2]

    return kernel


def near_kernel(rows, half, channels, width, space_n):
    def kernel(x_own, halo, *refs):
        w1, wf, wb, w1t, far_out = refs[:5]
        edges, (e1, e2) = refs[5:15], refs[15:17]
        t_rows, out = refs[17:19]
        xs, s1, s2 = refs[19:22]
        g3, work = refs[22], refs[23:]
        space, side, _ = place_on_mesh()
        exists = jnp.where(side == 0, space, space_n - 1 - space) > 0
        row_of = lambda local: jnp.where(side == 0, local, rows - 1 - local)
        place = lambda local: jnp.where(side == 0, local, half - 1 - local)
        spans = spans_of(half)[0]
        maps = [Maps(work[2 * i : 2 * i + 2], b) for i, b in enumerate((-5, -4, -4, -3, -2, -1))]
        a1, a2, _, d3, d2, d1 = maps
        for i, (m, row) in enumerate(((a1, 1), (a2, 2), (d3, 3), (d2, 4), (d1, 5))):
            m.load(edges[2 * i : 2 * i + 2], row, 2)
        s1[:, 2:6] = e1[...]
        s2[:, 4:6] = e2[...]
        for j in range(6, half):
            out[place(j)] = far_out[j - 6]

        def x_row(j):
            if j < 0:
                return halo[pl.ds(HALO_T * channels + 8 * (j + HALO_X), 8), :]
            return x_own[:, row_of(j), :]

        def t_row(j):
            if j < 0:
                return halo[pl.ds(channels * (j + HALO_T), channels), :]
            return t_rows[j]

        def keep(value, j):
            return jnp.where(exists, value, 0.0) if j < 0 else value

        def emit(j, value):
            out[place(j)] = value

        run(
            spans, (w1, wf, wb, w1t), xs, -6, maps, (s1, -1, s2, -2),
            x_row, t_row, keep, emit, channels, width, g3,
        )

    return kernel


def body(image, baseline, w_first, w_rest, target):
    colours, rows, width = image.shape
    channels = target.shape[0]
    half = rows // 2
    space_n, step_n = lax.axis_size("space"), lax.axis_size("step")
    step = lax.axis_index("step")
    side = step % 2
    in_hbm = lambda array: pltpu.with_memory_space_constraint(array, pltpu.HBM)
    target_hbm = in_hbm(target)
    w_taps = w_rest.transpose(0, 3, 4, 1, 2)
    params = pltpu.CompilerParams(vmem_limit_bytes=40 << 20)
    shape = jax.ShapeDtypeStruct

    x_own, send = pl.pallas_call(
        pack_kernel(rows, step_n),
        out_shape=(shape((8, rows, width), F32), shape((HALO_T * channels + HALO_X * 8, width), F32)),
        in_specs=[HBM, HBM, HBM],
        out_specs=(VMEM, VMEM),
        scratch_shapes=[pltpu.VMEM((colours, rows, width), F32)] * 2
        + [pltpu.SemaphoreType.DMA((2,)), pltpu.SemaphoreType.DMA((HALO_T,))],
        compiler_params=params,
        name="pack_edges",
    )(in_hbm(image), in_hbm(baseline), target_hbm)

    pairs = []
    for i in range(space_n):
        for s in range(step_n):
            source = i + 1 if s % 2 else i - 1
            if 0 <= source < space_n:
                pairs.append((source * step_n + s, i * step_n + s))
    halo = lax.ppermute(send, ("space", "step"), pairs)

    n = 3 * channels
    weight_shapes = [
        shape((2 * channels, 288), BF16),
        shape((2, n, 3 * n), BF16),
        shape((3, n, 3 * n), BF16),
        shape((24, 3 * n), BF16),
    ]
    edge_shapes = [shape((2, 2, channels, width), BF16)] * 8 + [shape((1, 2, channels, width), BF16)] * 2
    edge_shapes += [shape((2, 4, channels, width), F32), shape((2, 2, channels, width), F32)]

    def scratch(x_rows, s1_rows, s2_rows, counts, landing=0):
        refs = [pltpu.VMEM((x_rows, 48, width), BF16)]
        refs += [pltpu.VMEM((2, r, channels, width), F32) for r in (s1_rows, s2_rows)]
        if landing:
            refs += [pltpu.SemaphoreType.DMA((landing,))]
        else:
            refs += [pltpu.VMEM((6, channels, width), F32)]
        for i, count in enumerate(counts):
            refs += [pltpu.VMEM((1 if i in (2, 5) else 2, count, channels, width), BF16)] * 2
        return refs

    far = pl.pallas_call(
        far_kernel(rows, half, channels, width),
        out_shape=(*weight_shapes, shape((half - 6, 8, width), F32), *edge_shapes, shape((half + 4, channels, width), F32)),
        in_specs=[VMEM, HBM, VMEM, VMEM],
        out_specs=(VMEM,) * 18,
        scratch_shapes=scratch(half + 6, half, half, (half + 4, half + 2, half + 2, half, half - 2, half - 4), half + 4),
        compiler_params=params,
        name="far_rows",
    )(x_own, target_hbm, w_taps, w_first.transpose(1, 2, 3, 0))

    y = pl.pallas_call(
        near_kernel(rows, half, channels, width, space_n),
        out_shape=shape((half, 8, width), F32),
        in_specs=[VMEM] * 20,
        out_specs=VMEM,
        scratch_shapes=scratch(8, 6, 6, (8,) * 6),
        compiler_params=params,
        name="near_rows",
    )(x_own, halo, *far)
    y = y.transpose(1, 0, 2)[:colours]

    def partner(k):
        return lax.ppermute(y, "step", [(i, i ^ k) for i in range(step_n)])

    difference = image - baseline
    if step_n == 4:
        mine, theirs = y + partner(2), partner(1) + partner(3)
        whole = jnp.where(side == 0, jnp.concatenate([mine, theirs], 1), jnp.concatenate([theirs, mine], 1))
    else:
        order = lax.broadcasted_iota(jnp.int32, (2, 1, 1, 1), 0)
        halves = lax.psum(jnp.where(order == side, y[None], 0.0), "step")
        whole = jnp.concatenate([halves[0], halves[1]], 1)
    return difference * whole / step_n


def solution(mesh):
    in_specs = (P(None, "space", None), P(None, "space", None), P(), P(), P(None, "space", None))
    out_specs = P(None, "space", None)
    return jax.shard_map(body, mesh=mesh, in_specs=in_specs, out_specs=out_specs, check_vma=False)
```

```python
import functools

import jax
import jax.numpy as jnp
from jax import lax
from jax.experimental import pallas as pl
from jax.experimental.pallas import tpu as pltpu
from jax.sharding import PartitionSpec as P

F32, BF16 = jnp.float32, jnp.bfloat16
HALO_X, HALO_T = 6, 4
VMEM = pl.BlockSpec(memory_space=pltpu.VMEM)
HBM = pl.BlockSpec(memory_space=pltpu.HBM)


def dot(a, b):
    return jnp.dot(a, b, preferred_element_type=F32)


def split(value):
    high = value.astype(BF16)
    return high, (value - high.astype(F32)).astype(BF16)


def shift_cols(value, by):
    width = value.shape[-1]
    rolled = pltpu.roll(value, by % width, 1)
    cut = 128 if by > 0 else width - 128
    left, right = rolled[:, :cut], rolled[:, cut:]
    col = lax.broadcasted_iota(jnp.int32, (value.shape[0], 128), 1)
    if by > 0:
        left = jnp.where(col == 0, 0.0, left)
    else:
        right = jnp.where(col == 127, 0.0, right)
    return jnp.concatenate([left, right], 1)


def combine(y, rows):
    return y[rows : 2 * rows] + shift_cols(y[:rows], 1) + shift_cols(y[2 * rows : 3 * rows], -1)


def silu_and_slope(pre):
    sig = 1.0 / (1.0 + jnp.exp(-pre))
    act = pre * sig
    return act, sig + act * (1.0 - sig)


def conv_row(weights, high, low, index):
    stack = lambda ref: ref[index : index + 3].reshape(3 * ref.shape[1], ref.shape[2])
    upper, lower = stack(high), stack(low)
    return dot(weights, jnp.concatenate([upper, upper, lower], 0))


class Maps:
    def __init__(self, refs, base):
        self.high, self.low = refs
        self.base = base

    def put(self, step, row, value):
        self.high[step, row - self.base], self.low[step, row - self.base] = split(value)

    def conv(self, weights, step, row):
        return conv_row(weights, self.high.at[step], self.low.at[step], row - 1 - self.base)

    def copy(self, refs, row, count):
        for part, ref in zip((self.high, self.low), refs):
            ref[...] = part[:, row - self.base : row - self.base + count]

    def load(self, refs, row, count):
        for part, ref in zip((self.high, self.low), refs):
            part[:, row - self.base : row - self.base + count] = ref[...]


def run(spans, weights, xs, x_base, maps, slopes, x_row, t_row, keep, emit, channels, width, g3=None, ready=None, blocks=()):
    w1, wf, wb, w1t = weights
    a1, a2, t, d3, d2, d1 = maps
    s1, s1_base, s2, s2_base = slopes
    rows = lambda name: range(spans[name][0], spans[name][1] + 1)
    inside = lambda name, row: spans[name][0] <= row <= spans[name][1]
    for j in rows("x"):
        x = x_row(j)
        taps = jnp.concatenate([shift_cols(x, 1), x, shift_cols(x, -1)], 0)
        high = taps.astype(BF16).astype(F32)
        xs[j - x_base] = jnp.concatenate([high, taps - high], 0).astype(BF16)
    def first(j):
        stack = xs[j - 1 - x_base : j + 2 - x_base].reshape(3 * xs.shape[1], width)
        pre = dot(w1[...], jnp.concatenate([stack, stack], 0))
        for s in range(2):
            act, slope = silu_and_slope(pre[s * channels : (s + 1) * channels])
            a1.put(s, j, keep(act, j))
            if inside("s1", j):
                s1[s, j - s1_base] = keep(slope, j)

    def second(j):
        for s in range(2):
            if blocks:
                blocks.pop(0)()
            act, slope = silu_and_slope(combine(a1.conv(wf[0], s, j), channels))
            a2.put(s, j, keep(act, j))
            if inside("s2", j):
                s2[s, j - s2_base] = keep(slope, j)

    def target_grad(j):
        return combine(t.conv(wb[2], 0, j), channels)

    def arrive():
        for j in rows("t"):
            t.put(0, j, t_row(j))

    firsts, seconds, thirds = list(rows("a1")), list(rows("a2")), list(rows("d3"))
    early = []
    if not ready:
        arrive()
    for i, j in enumerate(firsts):
        first(j)
        if ready and i == 2:
            ready[0]()
        if ready and i == 7:
            ready[1]()
            arrive()
        if not ready and thirds[i:]:
            g3[thirds[i] - thirds[0]] = target_grad(thirds[i])
            early.append(thirds[i])
        if i >= 3:
            second(seconds.pop(0))
    for j in seconds:
        second(j)
    while blocks:
        blocks.pop(0)()
    for j in thirds:
        grad = g3[j - thirds[0]] if j in early else target_grad(j)
        for s in range(2):
            _, slope = silu_and_slope(combine(a2.conv(wf[1], s, j), channels))
            d3.put(s, j, keep(grad * slope, j))
    for j in rows("d2"):
        for s in range(2):
            d2.put(s, j, combine(d3.conv(wb[1], s, j), channels) * s2[s, j - s2_base])
    for j in rows("d1"):
        grads = [combine(d2.conv(wb[0], s, j), channels) * s1[s, j - s1_base] for s in range(2)]
        d1.put(0, j, grads[0] + grads[1])
    for j in rows("out"):
        emit(j, combine(d1.conv(w1t[...], 0, j), 8))


def halves(value):
    high = value.astype(BF16).astype(F32)
    return high, value - high


def wide(value):
    high, low = halves(value)
    return jnp.concatenate([high, low, high], 1).astype(BF16)


def forward_block(tap, w, wf, layer, dx):
    channels = w.shape[-1]
    taps = jnp.concatenate([w[layer, tap(dy), dx] for dy in range(3)], 1)
    wf[layer, pl.ds(dx * channels, channels), :] = wide(taps)


def backward_block(tap, w, wb, layer, dx):
    channels = w.shape[-1]
    taps = jnp.concatenate([w[layer, tap(2 - dy), 2 - dx] for dy in range(3)], 0)
    wb[layer, pl.ds(dx * channels, channels), :] = wide(taps.T)


def prepare_first(tap, w_first, w1, w1t, channels, colours):
    zeros = lambda count: jnp.zeros((count, channels), F32)
    for s in range(2):
        fronts, backs = [], []
        for dy in range(3):
            slots = [
                jnp.concatenate([zeros(4)] * s + [w_first[:, tap(dy), dx, :], zeros(4 - colours)] + [zeros(4)] * (1 - s), 0)
                for dx in range(3)
            ]
            high, low = halves(jnp.concatenate(slots, 0))
            fronts += [high, high]
            backs += [low, jnp.zeros_like(low)]
        w1[pl.ds(s * channels, channels), :] = jnp.concatenate(fronts + backs, 0).T.astype(BF16)
    last = [
        jnp.concatenate(
            sum([[w_first[:, tap(2 - dy), 2 - dx, :], zeros(8 - colours)] for dx in range(3)], []), 0
        )
        for dy in range(3)
    ]
    w1t[...] = wide(jnp.concatenate(last, 1))


def place_on_mesh():
    step = lax.axis_index("step")
    return lax.axis_index("space"), lax.rem(step, 2), lax.div(step, 2)


def pack_kernel(rows, step_n):
    def kernel(image, baseline, target, x_own, send, image_copy, base_copy, sems, row_sems):
        _, side, group = place_on_mesh()
        fractions = [((2 * group + s).astype(F32) + 0.5) * (1.0 / step_n) for s in range(2)]
        channels = target.shape[0]
        copies = []
        for j in range(HALO_T):
            row = jnp.where(side == 0, rows - HALO_T + j, HALO_T - 1 - j)
            place = send.at[pl.ds(channels * j, channels), :]
            copies.append(pltpu.make_async_copy(target.at[:, row, :], place, row_sems.at[j]))
        for source, landing, i in ((image, image_copy, 0), (baseline, base_copy, 1)):
            copies.append(pltpu.make_async_copy(source, landing, sems.at[i]))
        for copy in copies:
            copy.start()
        copies[-2].wait()
        copies[-1].wait()
        base, difference = base_copy[...], image_copy[...] - base_copy[...]
        colours = base.shape[0]
        zero = jnp.zeros((4 - colours,) + base.shape[1:], F32)
        for s in range(2):
            x_own[pl.ds(4 * s, colours)] = base + fractions[s] * difference
            x_own[pl.ds(4 * s + colours, 4 - colours)] = zero
        for j in range(HALO_X):
            row = jnp.where(side == 0, rows - HALO_X + j, HALO_X - 1 - j)
            for s in range(2):
                place = HALO_T * channels + (2 * j + s) * colours
                send[pl.ds(place, colours), :] = x_own[pl.ds(4 * s, colours), row, :]
        for copy in copies[:-2]:
            copy.wait()

    return kernel


def spans_of(half):
    near = {"x": (-6, 1), "t": (-4, 3), "a1": (-5, 0), "s1": (-1, 0), "a2": (-4, 1), "s2": (-2, 1)}
    near |= {"d3": (-3, 2), "d2": (-2, 3), "d1": (-1, 4), "out": (0, 5)}
    far = {"x": (0, half + 5), "t": (2, half + 3), "a1": (1, half + 4), "s1": (1, half), "a2": (2, half + 3)}
    far |= {"s2": (2, half + 1), "d3": (3, half + 2), "d2": (4, half + 1), "d1": (5, half), "out": (6, half - 1)}
    return near, far


def fetch_rows(target, landing, sems, row_of):
    copies = []
    for local in range(landing.shape[0]):
        copies.append(pltpu.make_async_copy(target.at[:, row_of(local), :], landing.at[local], sems.at[local]))
        copies[-1].start()
    return lambda local: copies[local].wait()


def far_kernel(rows, half, channels, width):
    def kernel(x_own, target, w, w_first, *refs):
        w1, wf, wb, w1t, out = refs[:5]
        edges, (e1, e2) = refs[5:15], refs[15:17]
        t_rows = refs[17]
        xs, s1, s2, t_sems = refs[18:22]
        work = refs[22:]
        _, side, _ = place_on_mesh()
        row_of = lambda local: jnp.where(side == 0, local, rows - 1 - local)
        t_row = fetch_rows(target, t_rows, t_sems, row_of)
        tap = lambda dy: jnp.where(side == 1, 2 - dy, dy)
        prepare_first(tap, w_first, w1, w1t, channels, w_first.shape[0])
        backward = lambda layer: [functools.partial(backward_block, tap, w, wb, layer, dx) for dx in range(3)]
        blocks = backward(0)

        def ready():
            for dx in range(3):
                forward_block(tap, w, wf, 0, dx)

        def landed():
            for local in range(t_rows.shape[0]):
                t_row(local)
            blocks.extend(functools.partial(forward_block, tap, w, wf, 1, dx) for dx in range(3))
            blocks.extend(backward(2) + backward(1))

        spans = spans_of(half)[1]
        maps = [Maps(work[2 * i : 2 * i + 2], b) for i, b in enumerate((1, 2, 2, 3, 4, 5))]

        def emit(j, value):
            out[j - spans["out"][0]] = value

        run(
            spans, (w1, wf, wb, w1t), xs, 0, maps, (s1, 1, s2, 2),
            lambda j: x_own[:, row_of(j), :], lambda j: t_rows[j],
            lambda value, j: value, emit, channels, width, None, (ready, landed), blocks,
        )
        a1, a2, _, d3, d2, d1 = maps
        for i, (m, row) in enumerate(((a1, 1), (a2, 2), (d3, 3), (d2, 4), (d1, 5))):
            m.copy(edges[2 * i : 2 * i + 2], row, 2)
        e1[...] = s1[:, 0:4]
        e2[...] = s2[:, 0:2]

    return kernel


def near_kernel(rows, half, channels, width, space_n, colours):
    def kernel(x_own, halo, *refs):
        w1, wf, wb, w1t, far_out = refs[:5]
        edges, (e1, e2) = refs[5:15], refs[15:17]
        t_rows, out = refs[17:19]
        xs, s1, s2 = refs[19:22]
        g3, work = refs[22], refs[23:]
        space, side, _ = place_on_mesh()
        exists = jnp.where(side == 0, space, space_n - 1 - space) > 0
        row_of = lambda local: jnp.where(side == 0, local, rows - 1 - local)
        place = lambda local: jnp.where(side == 0, local, half - 1 - local)
        spans = spans_of(half)[0]
        maps = [Maps(work[2 * i : 2 * i + 2], b) for i, b in enumerate((-5, -4, -4, -3, -2, -1))]
        a1, a2, _, d3, d2, d1 = maps
        for i, (m, row) in enumerate(((a1, 1), (a2, 2), (d3, 3), (d2, 4), (d1, 5))):
            m.load(edges[2 * i : 2 * i + 2], row, 2)
        s1[:, 2:6] = e1[...]
        s2[:, 4:6] = e2[...]
        for j in range(6, half):
            out[place(j)] = far_out[j - 6]

        def x_row(j):
            if j < 0:
                first = HALO_T * channels + 2 * (j + HALO_X) * colours
                zero = jnp.zeros((4 - colours, width), F32)
                pieces = [halo[pl.ds(first + s * colours, colours), :] for s in range(2)]
                return jnp.concatenate([pieces[0], zero, pieces[1], zero], 0)
            return x_own[:, row_of(j), :]

        def t_row(j):
            if j < 0:
                return halo[pl.ds(channels * (j + HALO_T), channels), :]
            return t_rows[j]

        def keep(value, j):
            return jnp.where(exists, value, 0.0) if j < 0 else value

        def emit(j, value):
            out[place(j)] = value

        run(
            spans, (w1, wf, wb, w1t), xs, -6, maps, (s1, -1, s2, -2),
            x_row, t_row, keep, emit, channels, width, g3,
        )

    return kernel


def body(image, baseline, w_first, w_rest, target):
    colours, rows, width = image.shape
    channels = target.shape[0]
    half = rows // 2
    space_n, step_n = lax.axis_size("space"), lax.axis_size("step")
    step = lax.axis_index("step")
    side = step % 2
    in_hbm = lambda array: pltpu.with_memory_space_constraint(array, pltpu.HBM)
    target_hbm = in_hbm(target)
    w_taps = w_rest.transpose(0, 3, 4, 1, 2)
    params = pltpu.CompilerParams(vmem_limit_bytes=40 << 20)
    shape = jax.ShapeDtypeStruct

    x_own, send = pl.pallas_call(
        pack_kernel(rows, step_n),
        out_shape=(shape((8, rows, width), F32), shape((HALO_T * channels + HALO_X * 2 * colours, width), F32)),
        in_specs=[HBM, HBM, HBM],
        out_specs=(VMEM, VMEM),
        scratch_shapes=[pltpu.VMEM((colours, rows, width), F32)] * 2
        + [pltpu.SemaphoreType.DMA((2,)), pltpu.SemaphoreType.DMA((HALO_T,))],
        compiler_params=params,
        name="pack_edges",
    )(in_hbm(image), in_hbm(baseline), target_hbm)

    pairs = []
    for i in range(space_n):
        for s in range(step_n):
            source = i + 1 if s % 2 else i - 1
            if 0 <= source < space_n:
                pairs.append((source * step_n + s, i * step_n + s))
    halo = lax.ppermute(send, ("space", "step"), pairs)

    n = 3 * channels
    weight_shapes = [
        shape((2 * channels, 288), BF16),
        shape((2, n, 3 * n), BF16),
        shape((3, n, 3 * n), BF16),
        shape((24, 3 * n), BF16),
    ]
    edge_shapes = [shape((2, 2, channels, width), BF16)] * 8 + [shape((1, 2, channels, width), BF16)] * 2
    edge_shapes += [shape((2, 4, channels, width), F32), shape((2, 2, channels, width), F32)]

    def scratch(x_rows, s1_rows, s2_rows, counts, landing=0):
        refs = [pltpu.VMEM((x_rows, 48, width), BF16)]
        refs += [pltpu.VMEM((2, r, channels, width), F32) for r in (s1_rows, s2_rows)]
        if landing:
            refs += [pltpu.SemaphoreType.DMA((landing,))]
        else:
            refs += [pltpu.VMEM((6, channels, width), F32)]
        for i, count in enumerate(counts):
            refs += [pltpu.VMEM((1 if i in (2, 5) else 2, count, channels, width), BF16)] * 2
        return refs

    far = pl.pallas_call(
        far_kernel(rows, half, channels, width),
        out_shape=(*weight_shapes, shape((half - 6, 8, width), F32), *edge_shapes, shape((half + 4, channels, width), F32)),
        in_specs=[VMEM, HBM, VMEM, VMEM],
        out_specs=(VMEM,) * 18,
        scratch_shapes=scratch(half + 6, half, half, (half + 4, half + 2, half + 2, half, half - 2, half - 4), half + 4),
        compiler_params=params,
        name="far_rows",
    )(x_own, target_hbm, w_taps, w_first.transpose(1, 2, 3, 0))

    y = pl.pallas_call(
        near_kernel(rows, half, channels, width, space_n, colours),
        out_shape=shape((half, 8, width), F32),
        in_specs=[VMEM] * 20,
        out_specs=VMEM,
        scratch_shapes=scratch(8, 6, 6, (8,) * 6),
        compiler_params=params,
        name="near_rows",
    )(x_own, halo, *far)
    y = y.transpose(1, 0, 2)[:colours]

    def partner(k):
        return lax.ppermute(y, "step", [(i, i ^ k) for i in range(step_n)])

    difference = image - baseline
    if step_n == 4:
        mine, theirs = y + partner(2), partner(1) + partner(3)
        whole = jnp.where(side == 0, jnp.concatenate([mine, theirs], 1), jnp.concatenate([theirs, mine], 1))
    else:
        order = lax.broadcasted_iota(jnp.int32, (2, 1, 1, 1), 0)
        halves = lax.psum(jnp.where(order == side, y[None], 0.0), "step")
        whole = jnp.concatenate([halves[0], halves[1]], 1)
    return difference * whole / step_n


def solution(mesh):
    in_specs = (P(None, "space", None), P(None, "space", None), P(), P(), P(None, "space", None))
    out_specs = P(None, "space", None)
    return jax.shard_map(body, mesh=mesh, in_specs=in_specs, out_specs=out_specs, check_vma=False)
```

```python
import functools

import jax
import jax.numpy as jnp
from jax import lax
from jax.experimental import pallas as pl
from jax.experimental.pallas import tpu as pltpu
from jax.sharding import PartitionSpec as P

F32, BF16 = jnp.float32, jnp.bfloat16
HALO_X, HALO_T = 6, 4
VMEM = pl.BlockSpec(memory_space=pltpu.VMEM)
HBM = pl.BlockSpec(memory_space=pltpu.HBM)


def dot(a, b):
    return jnp.dot(a, b, preferred_element_type=F32)


def split(value):
    high = value.astype(BF16)
    return high, (value - high.astype(F32)).astype(BF16)


def shift_cols(value, by):
    width = value.shape[-1]
    rolled = pltpu.roll(value, by % width, 1)
    cut = 128 if by > 0 else width - 128
    left, right = rolled[:, :cut], rolled[:, cut:]
    col = lax.broadcasted_iota(jnp.int32, (value.shape[0], 128), 1)
    if by > 0:
        left = jnp.where(col == 0, 0.0, left)
    else:
        right = jnp.where(col == 127, 0.0, right)
    return jnp.concatenate([left, right], 1)


def combine(y, rows):
    return y[rows : 2 * rows] + shift_cols(y[:rows], 1) + shift_cols(y[2 * rows : 3 * rows], -1)


def silu_and_slope(pre):
    sig = 1.0 / (1.0 + jnp.exp(-pre))
    act = pre * sig
    return act, sig + act * (1.0 - sig)


def conv_row(weights, high, low, index):
    stack = lambda ref: ref[index : index + 3].reshape(3 * ref.shape[1], ref.shape[2])
    upper, lower = stack(high), stack(low)
    return dot(weights, jnp.concatenate([upper, upper, lower], 0))


class Maps:
    def __init__(self, refs, base):
        self.high, self.low = refs
        self.base = base

    def put(self, step, row, value):
        self.high[step, row - self.base], self.low[step, row - self.base] = split(value)

    def conv(self, weights, step, row):
        return conv_row(weights, self.high.at[step], self.low.at[step], row - 1 - self.base)

    def copy(self, refs, row, count):
        for part, ref in zip((self.high, self.low), refs):
            ref[...] = part[:, row - self.base : row - self.base + count]

    def load(self, refs, row, count):
        for part, ref in zip((self.high, self.low), refs):
            part[:, row - self.base : row - self.base + count] = ref[...]


def run(spans, weights, xs, x_base, maps, slopes, x_row, t_row, keep, emit, channels, width, g3=None, ready=None, blocks=()):
    w1, wf, wb, w1t = weights
    a1, a2, t, d3, d2, d1 = maps
    s1, s1_base, s2, s2_base = slopes
    rows = lambda name: range(spans[name][0], spans[name][1] + 1)
    inside = lambda name, row: spans[name][0] <= row <= spans[name][1]
    for j in rows("x"):
        x = x_row(j)
        taps = jnp.concatenate([shift_cols(x, 1), x, shift_cols(x, -1)], 0)
        high = taps.astype(BF16).astype(F32)
        xs[j - x_base] = jnp.concatenate([high, taps - high], 0).astype(BF16)
    def first(j):
        stack = xs[j - 1 - x_base : j + 2 - x_base].reshape(3 * xs.shape[1], width)
        pre = dot(w1[...], jnp.concatenate([stack, stack], 0))
        for s in range(2):
            act, slope = silu_and_slope(pre[s * channels : (s + 1) * channels])
            a1.put(s, j, keep(act, j))
            if inside("s1", j):
                s1[s, j - s1_base] = keep(slope, j)

    def second(j):
        for s in range(2):
            if blocks:
                blocks.pop(0)()
            act, slope = silu_and_slope(combine(a1.conv(wf[0], s, j), channels))
            a2.put(s, j, keep(act, j))
            if inside("s2", j):
                s2[s, j - s2_base] = keep(slope, j)

    def target_grad(j):
        return combine(t.conv(wb[2], 0, j), channels)

    def arrive():
        for j in rows("t"):
            t.put(0, j, t_row(j))

    firsts, seconds, thirds = list(rows("a1")), list(rows("a2")), list(rows("d3"))
    early = []
    if not ready:
        arrive()
    for i, j in enumerate(firsts):
        first(j)
        if ready and i == 2:
            ready[0]()
        if ready and i == 7:
            ready[1]()
            arrive()
        if not ready and thirds[i:]:
            g3[thirds[i] - thirds[0]] = target_grad(thirds[i])
            early.append(thirds[i])
        if i >= 3:
            second(seconds.pop(0))
    for j in seconds:
        second(j)
    while blocks:
        blocks.pop(0)()
    for j in thirds:
        grad = g3[j - thirds[0]] if j in early else target_grad(j)
        for s in range(2):
            _, slope = silu_and_slope(combine(a2.conv(wf[1], s, j), channels))
            d3.put(s, j, keep(grad * slope, j))
    for j in rows("d2"):
        for s in range(2):
            d2.put(s, j, combine(d3.conv(wb[1], s, j), channels) * s2[s, j - s2_base])
    for j in rows("d1"):
        grads = [combine(d2.conv(wb[0], s, j), channels) * s1[s, j - s1_base] for s in range(2)]
        d1.put(0, j, grads[0] + grads[1])
    for j in rows("out"):
        emit(j, combine(d1.conv(w1t[...], 0, j), 8))


def halves(value):
    high = value.astype(BF16).astype(F32)
    return high, value - high


def wide(value):
    high, low = halves(value)
    return jnp.concatenate([high, low, high], 1).astype(BF16)


def forward_block(tap, w, wf, layer, dx):
    channels = w.shape[-1]
    taps = jnp.concatenate([w[layer, tap(dy), dx] for dy in range(3)], 1)
    wf[layer, pl.ds(dx * channels, channels), :] = wide(taps)


def backward_block(tap, w, wb, layer, dx):
    channels = w.shape[-1]
    taps = jnp.concatenate([w[layer, tap(2 - dy), 2 - dx] for dy in range(3)], 0)
    wb[layer, pl.ds(dx * channels, channels), :] = wide(taps.T)


def prepare_first(tap, w_first, w1, w1t, channels, colours):
    zeros = lambda count: jnp.zeros((count, channels), F32)
    for s in range(2):
        fronts, backs = [], []
        for dy in range(3):
            slots = [
                jnp.concatenate([zeros(4)] * s + [w_first[:, tap(dy), dx, :], zeros(4 - colours)] + [zeros(4)] * (1 - s), 0)
                for dx in range(3)
            ]
            high, low = halves(jnp.concatenate(slots, 0))
            fronts += [high, high]
            backs += [low, jnp.zeros_like(low)]
        w1[pl.ds(s * channels, channels), :] = jnp.concatenate(fronts + backs, 0).T.astype(BF16)
    last = [
        jnp.concatenate(
            sum([[w_first[:, tap(2 - dy), 2 - dx, :], zeros(8 - colours)] for dx in range(3)], []), 0
        )
        for dy in range(3)
    ]
    w1t[...] = wide(jnp.concatenate(last, 1))


def place_on_mesh():
    step = lax.axis_index("step")
    return lax.axis_index("space"), lax.rem(step, 2), lax.div(step, 2)


def pack_kernel(rows, step_n):
    def kernel(image, baseline, target, x_own, send, image_copy, base_copy, sems, row_sems):
        _, side, group = place_on_mesh()
        fractions = [((2 * group + s).astype(F32) + 0.5) * (1.0 / step_n) for s in range(2)]
        channels = target.shape[0]
        copies = []
        for j in range(HALO_T):
            row = jnp.where(side == 0, rows - HALO_T + j, HALO_T - 1 - j)
            place = send.at[pl.ds(channels * j, channels), :]
            copies.append(pltpu.make_async_copy(target.at[:, row, :], place, row_sems.at[j]))
        for source, landing, i in ((image, image_copy, 0), (baseline, base_copy, 1)):
            copies.append(pltpu.make_async_copy(source, landing, sems.at[i]))
        for copy in copies:
            copy.start()
        copies[-2].wait()
        copies[-1].wait()
        base, difference = base_copy[...], image_copy[...] - base_copy[...]
        colours = base.shape[0]
        zero = jnp.zeros((4 - colours,) + base.shape[1:], F32)
        for s in range(2):
            x_own[pl.ds(4 * s, colours)] = base + fractions[s] * difference
            x_own[pl.ds(4 * s + colours, 4 - colours)] = zero
        for j in range(HALO_X):
            row = jnp.where(side == 0, rows - HALO_X + j, HALO_X - 1 - j)
            for s in range(2):
                place = HALO_T * channels + (2 * j + s) * colours
                send[pl.ds(place, colours), :] = x_own[pl.ds(4 * s, colours), row, :]
        for copy in copies[:-2]:
            copy.wait()

    return kernel


def spans_of(half):
    near = {"x": (-6, 1), "t": (-4, 3), "a1": (-5, 0), "s1": (-1, 0), "a2": (-4, 1), "s2": (-2, 1)}
    near |= {"d3": (-3, 2), "d2": (-2, 3), "d1": (-1, 4), "out": (0, 5)}
    far = {"x": (0, half + 5), "t": (2, half + 3), "a1": (1, half + 4), "s1": (1, half), "a2": (2, half + 3)}
    far |= {"s2": (2, half + 1), "d3": (3, half + 2), "d2": (4, half + 1), "d1": (5, half), "out": (6, half - 1)}
    return near, far


def fetch_rows(target, landing, sems, row_of):
    copies = []
    for local in range(landing.shape[0]):
        copies.append(pltpu.make_async_copy(target.at[:, row_of(local), :], landing.at[local], sems.at[local]))
        copies[-1].start()
    return lambda local: copies[local].wait()


def far_kernel(rows, half, channels, width):
    def kernel(x_own, target, w, w_first, *refs):
        w1, wf, wb, w1t, out = refs[:5]
        edges, (e1, e2) = refs[5:15], refs[15:17]
        t_rows = refs[17]
        xs, s1, s2, t_sems = refs[18:22]
        work = refs[22:]
        _, side, _ = place_on_mesh()
        row_of = lambda local: jnp.where(side == 0, local, rows - 1 - local)
        t_row = fetch_rows(target, t_rows, t_sems, row_of)
        tap = lambda dy: jnp.where(side == 1, 2 - dy, dy)
        prepare_first(tap, w_first, w1, w1t, channels, w_first.shape[0])
        backward = lambda layer: [functools.partial(backward_block, tap, w, wb, layer, dx) for dx in range(3)]
        blocks = backward(0)

        def ready():
            for dx in range(3):
                forward_block(tap, w, wf, 0, dx)

        def landed():
            for local in range(t_rows.shape[0]):
                t_row(local)
            blocks.extend(functools.partial(forward_block, tap, w, wf, 1, dx) for dx in range(3))
            blocks.extend(backward(2) + backward(1))

        spans = spans_of(half)[1]
        maps = [Maps(work[2 * i : 2 * i + 2], b) for i, b in enumerate((1, 2, 2, 3, 4, 5))]

        def emit(j, value):
            out[j - spans["out"][0]] = value

        run(
            spans, (w1, wf, wb, w1t), xs, 0, maps, (s1, 1, s2, 2),
            lambda j: x_own[:, row_of(j), :], lambda j: t_rows[j],
            lambda value, j: value, emit, channels, width, None, (ready, landed), blocks,
        )
        a1, a2, _, d3, d2, d1 = maps
        for i, (m, row) in enumerate(((a1, 1), (a2, 2), (d3, 3), (d2, 4), (d1, 5))):
            m.copy(edges[2 * i : 2 * i + 2], row, 2)
        e1[...] = s1[:, 0:4]
        e2[...] = s2[:, 0:2]

    return kernel


def near_kernel(rows, half, channels, width, space_n, colours):
    def kernel(x_own, halo, *refs):
        w1, wf, wb, w1t, far_out = refs[:5]
        edges, (e1, e2) = refs[5:15], refs[15:17]
        t_rows, out = refs[17:19]
        xs, s1, s2 = refs[19:22]
        g3, work = refs[22], refs[23:]
        space, side, _ = place_on_mesh()
        exists = jnp.where(side == 0, space, space_n - 1 - space) > 0
        row_of = lambda local: jnp.where(side == 0, local, rows - 1 - local)
        place = lambda local: jnp.where(side == 0, local, half - 1 - local)
        spans = spans_of(half)[0]
        maps = [Maps(work[2 * i : 2 * i + 2], b) for i, b in enumerate((-5, -4, -4, -3, -2, -1))]
        a1, a2, _, d3, d2, d1 = maps
        for i, (m, row) in enumerate(((a1, 1), (a2, 2), (d3, 3), (d2, 4), (d1, 5))):
            m.load(edges[2 * i : 2 * i + 2], row, 2)
        s1[:, 2:6] = e1[...]
        s2[:, 4:6] = e2[...]
        for j in range(6, half):
            out[place(j)] = far_out[j - 6]

        def x_row(j):
            if j < 0:
                first = HALO_T * channels + 2 * (j + HALO_X) * colours
                zero = jnp.zeros((4 - colours, width), F32)
                pieces = [halo[pl.ds(first + s * colours, colours), :] for s in range(2)]
                return jnp.concatenate([pieces[0], zero, pieces[1], zero], 0)
            return x_own[:, row_of(j), :]

        def t_row(j):
            if j < 0:
                return halo[pl.ds(channels * (j + HALO_T), channels), :]
            return t_rows[j]

        def keep(value, j):
            return jnp.where(exists, value, 0.0) if j < 0 else value

        def emit(j, value):
            out[place(j)] = value

        run(
            spans, (w1, wf, wb, w1t), xs, -6, maps, (s1, -1, s2, -2),
            x_row, t_row, keep, emit, channels, width, g3,
        )

    return kernel


def body(image, baseline, w_first, w_rest, target):
    colours, rows, width = image.shape
    channels = target.shape[0]
    half = rows // 2
    space_n, step_n = lax.axis_size("space"), lax.axis_size("step")
    step = lax.axis_index("step")
    side = step % 2
    in_hbm = lambda array: pltpu.with_memory_space_constraint(array, pltpu.HBM)
    target_hbm = in_hbm(target)
    w_taps = w_rest.transpose(0, 3, 4, 1, 2)
    params = pltpu.CompilerParams(vmem_limit_bytes=40 << 20)
    shape = jax.ShapeDtypeStruct

    x_own, send = pl.pallas_call(
        pack_kernel(rows, step_n),
        out_shape=(shape((8, rows, width), F32), shape((HALO_T * channels + HALO_X * 2 * colours, width), F32)),
        in_specs=[HBM, HBM, HBM],
        out_specs=(VMEM, VMEM),
        scratch_shapes=[pltpu.VMEM((colours, rows, width), F32)] * 2
        + [pltpu.SemaphoreType.DMA((2,)), pltpu.SemaphoreType.DMA((HALO_T,))],
        compiler_params=params,
        name="pack_edges",
    )(in_hbm(image), in_hbm(baseline), target_hbm)

    pairs = []
    for i in range(space_n):
        for s in range(step_n):
            source = i + 1 if s % 2 else i - 1
            if 0 <= source < space_n:
                pairs.append((source * step_n + s, i * step_n + s))
    halo = lax.ppermute(send, ("space", "step"), pairs)

    n = 3 * channels
    weight_shapes = [
        shape((2 * channels, 288), BF16),
        shape((2, n, 3 * n), BF16),
        shape((3, n, 3 * n), BF16),
        shape((24, 3 * n), BF16),
    ]
    edge_shapes = [shape((2, 2, channels, width), BF16)] * 8 + [shape((1, 2, channels, width), BF16)] * 2
    edge_shapes += [shape((2, 4, channels, width), F32), shape((2, 2, channels, width), F32)]

    def scratch(x_rows, s1_rows, s2_rows, counts, landing=0):
        refs = [pltpu.VMEM((x_rows, 48, width), BF16)]
        refs += [pltpu.VMEM((2, r, channels, width), F32) for r in (s1_rows, s2_rows)]
        if landing:
            refs += [pltpu.SemaphoreType.DMA((landing,))]
        else:
            refs += [pltpu.VMEM((6, channels, width), F32)]
        for i, count in enumerate(counts):
            refs += [pltpu.VMEM((1 if i in (2, 5) else 2, count, channels, width), BF16)] * 2
        return refs

    far = pl.pallas_call(
        far_kernel(rows, half, channels, width),
        out_shape=(*weight_shapes, shape((half - 6, 8, width), F32), *edge_shapes, shape((half + 4, channels, width), F32)),
        in_specs=[VMEM, HBM, VMEM, VMEM],
        out_specs=(VMEM,) * 18,
        scratch_shapes=scratch(half + 6, half, half, (half + 4, half + 2, half + 2, half, half - 2, half - 4), half + 4),
        compiler_params=params,
        name="far_rows",
    )(x_own, target_hbm, w_taps, w_first.transpose(1, 2, 3, 0))

    y = pl.pallas_call(
        near_kernel(rows, half, channels, width, space_n, colours),
        out_shape=shape((half, 8, width), F32),
        in_specs=[VMEM] * 20,
        out_specs=VMEM,
        scratch_shapes=scratch(8, 6, 6, (8,) * 6),
        compiler_params=params,
        name="near_rows",
    )(x_own, halo, *far)
    y = y.transpose(1, 0, 2)[:colours]

    def partner(value, k):
        return lax.ppermute(value, "step", [(i, i ^ k) for i in range(step_n)])

    difference = image - baseline
    if step_n == 4:
        mine = y + partner(y, 2)
        theirs = partner(mine, 1)
        whole = jnp.where(side == 0, jnp.concatenate([mine, theirs], 1), jnp.concatenate([theirs, mine], 1))
    else:
        order = lax.broadcasted_iota(jnp.int32, (2, 1, 1, 1), 0)
        halves = lax.psum(jnp.where(order == side, y[None], 0.0), "step")
        whole = jnp.concatenate([halves[0], halves[1]], 1)
    return difference * whole / step_n


def solution(mesh):
    in_specs = (P(None, "space", None), P(None, "space", None), P(), P(), P(None, "space", None))
    out_specs = P(None, "space", None)
    return jax.shard_map(body, mesh=mesh, in_specs=in_specs, out_specs=out_specs, check_vma=False)
```
